256 devices in a mesh: seq: 32 (over x, z), head: 8 (over y, core).
Axes of the slice: x: 4, y: 4, z: 8, core: 2. Of those that a mesh axis runs over, the one named last changes fastest.
Arguments:
- hidden_states: bfloat16 [16384, 2048], P('seq', 'head'), may hold values from -7 to 7
- proj_ba: bfloat16 [2048, 64], P('head'), may hold values from -0.125 to 0.125
- query_in: bfloat16 [16384, 2048], P('seq', 'head'), may hold values from -6 to 6
- key_in: bfloat16 [16384, 2048], P('seq', 'head'), may hold values from -6 to 6
- value_in: bfloat16 [16384, 4096], P('seq', 'head'), may hold values from -6 to 6
- conv_query: bfloat16 [4, 2048], P(None, 'head'), may hold values from -2 to 2
- conv_key: bfloat16 [4, 2048], P(None, 'head'), may hold values from -2 to 2
- convolution_value_taps: bfloat16 [4, 4096], P(None, 'head'), may hold values from -2.5 to 2.5
- decay_scale: float32 [32], P('head'), may hold values from 1 to 16
- dt_bias: float32 [32], P('head'), may hold values from -30 to -2
Outputs:
- layer_output: float32 [16384, 4096], P('seq', 'head')
The draws below stay inside these ranges and needn't reach their ends.
All inputs are finite; a program needn't handle non-finite values.
Results may differ from the reference program's by a relative error of at most 0.0003.
Values may be sent and summed in bfloat16 or wider, within the bound.
A program may use at most 128 MiB of HBM per device.

```python
import math
import jax
import jax.numpy as jnp
from jax import lax

D = 2048
HK = 16
HV = 32
DK = 128
DV = 128
KCONV = 4
BLOCK = 128
TOKENS = 16384


def sudden_sign_flip(key):
    coin_flips = jax.random.bernoulli(jax.random.fold_in(key, 11), 0.5, (D,))
    return jnp.where(coin_flips, 1.0, -1.0).astype(jnp.float32)


def draw_hidden_states(key, part):
    row_of_signs = sudden_sign_flip(key)
    normal_part = jax.random.normal(jax.random.fold_in(key, 1), (TOKENS, D), jnp.float32)
    places = jax.random.randint(jax.random.fold_in(key, 2), (8,), 0, TOKENS)
    row_ids = jnp.arange(TOKENS)[:, None]
    marked = jnp.any(row_ids == places[None, :], axis=1)[:, None]
    blended = jnp.where(marked, 0.3 * normal_part + 4.0 * row_of_signs[None, :], normal_part)
    return jnp.clip(blended, -7.0, 7.0).astype(jnp.bfloat16)


def draw_proj_ba(key, part):
    row_of_signs = sudden_sign_flip(key)
    random_part = jax.random.normal(jax.random.fold_in(key, 4), (D, 2 * HV), jnp.float32)
    column_ids = jnp.arange(2 * HV)
    is_gate = jnp.where(column_ids % 2 == 0, 1.0, 0.0)[None, :]
    planted = 2.25 * row_of_signs[:, None] * is_gate / D
    return jnp.clip(random_part / math.sqrt(D) + planted, -0.125, 0.125).astype(jnp.bfloat16)


def convolution_taps(key, salt_value):
    channel_scale = jnp.exp(jax.random.uniform(jax.random.fold_in(key, salt_value), (HK * DK,), jnp.float32, math.log(0.02), 0.0))
    tap_values = 0.5 * jax.random.normal(jax.random.fold_in(key, salt_value + 1), (KCONV, HK * DK), jnp.float32)
    return jnp.clip(tap_values * channel_scale[None, :], -2.0, 2.0).astype(jnp.bfloat16)


def draw_conv_query(key, part):
    return convolution_taps(key, 31)


def draw_conv_key(key, part):
    return convolution_taps(key, 41)


def draw_dt_bias(key, part):
    lowest = math.log(1.0 / (16.0 * TOKENS))
    slow_share = 0.5
    slow_mask = jax.random.bernoulli(jax.random.fold_in(key, 21), slow_share, (HV,))
    slow_value = lowest + jax.random.uniform(jax.random.fold_in(key, 22), (HV,), jnp.float32, 0.0, 2.0)
    fast_value = jax.random.uniform(jax.random.fold_in(key, 23), (HV,), jnp.float32, -4.5, -3.0)
    return jnp.where(slow_mask, slow_value, fast_value).astype(jnp.float32)


def block_scale(rng, dims, split, least, largest):
    loudness = 1.0
    for axis_at, shards_of in split:
        steps = jax.random.uniform(jax.random.fold_in(jax.random.fold_in(rng, 6), axis_at), (shards_of,), jnp.float32, least / len(split), largest / len(split))
        loudness = loudness * jnp.repeat(jnp.exp(steps), dims[axis_at] // shards_of).reshape((-1,) + (1,) * (len(dims) - 1 - axis_at))
    return loudness


def gaussian(stream_key, dims, width, limit, cuts=(), held_as=jnp.bfloat16):
    entries = width * jax.random.normal(stream_key, dims, jnp.float32)
    if cuts:
        entries = entries * block_scale(stream_key, dims, cuts, -0.22, 0.18)
    return jnp.clip(entries, -limit, limit).astype(held_as)


def setup_inputs(seed: int = 0) -> dict:
    keys = jax.random.split(jax.random.key(seed), 11)
    return {
        "hidden_states": draw_hidden_states(jax.random.fold_in(keys[10], 71), 0),
        "proj_ba": draw_proj_ba(jax.random.fold_in(keys[10], 71), 0),
        "query_in": gaussian(keys[2], (TOKENS, HK * DK), 1.0, 6.0, ((0, 32), (1, 8))),
        "key_in": gaussian(keys[3], (TOKENS, HK * DK), 1.0, 6.0, ((0, 32), (1, 8))),
        "value_in": gaussian(keys[4], (TOKENS, HV * DV), 1.0, 6.0, ((0, 32), (1, 8))),
        "conv_query": draw_conv_query(jax.random.fold_in(keys[10], 71), 0),
        "conv_key": draw_conv_key(jax.random.fold_in(keys[10], 71), 0),
        "convolution_value_taps": gaussian(keys[7], (KCONV, HV * DV), 0.5, 2.5, ((1, 8),)),
        "decay_scale": jnp.clip(jnp.exp(math.log(16.0) - 2.7725887 * jax.random.uniform(keys[8], (HV,), jnp.float32) ** block_scale(keys[8], (HV,), ((0, 8),), -0.2, 0.2)), 1.0, 16.0),
        "dt_bias": draw_dt_bias(jax.random.fold_in(keys[10], 71), 0),
    }


highest = lax.Precision.HIGHEST

def causal_conv(inputs, weights):
    padded = jnp.pad(inputs.astype(jnp.float32), ((KCONV - 1, 0), (0, 0)))
    length = inputs.shape[0]
    kernel = weights.astype(jnp.float32)
    summed = jnp.zeros((length, inputs.shape[1]), jnp.float32)
    for offset in range(KCONV):
        summed = summed + kernel[offset][None, :] * lax.slice_in_dim(padded, offset, offset + length, axis=0)
    return jax.nn.silu(summed)

def unit_norm(features, factor):
    return features * lax.rsqrt(lax.optimization_barrier(jnp.sum(features * features, axis=-1, keepdims=True)) + 1e-06) * factor

def block_terms(queries, key_rows, values, log_decay, write_rate):
    block_length = queries.shape[-2]
    cumulative = jnp.cumsum(log_decay, axis=-1)
    row_index = lax.broadcasted_iota(jnp.int32, (block_length, block_length), 0)
    column_index = lax.broadcasted_iota(jnp.int32, (block_length, block_length), 1)
    causal = row_index >= column_index
    strict = row_index > column_index
    spread = cumulative[..., :, None] - cumulative[..., None, :]
    decay_table = jnp.where(causal, jnp.exp(jnp.where(causal, spread, 0.0)), 0.0)
    key_dots = jnp.einsum('...td,...sd->...ts', key_rows, key_rows, precision=highest)
    lower_part = jnp.where(strict, write_rate[..., :, None] * decay_table * key_dots, 0.0)
    system = lower_part + jnp.eye(block_length, dtype=jnp.float32)
    growth = jnp.exp(cumulative)
    stacked = jnp.concatenate([write_rate[..., None] * values, (write_rate * growth)[..., None] * key_rows], axis=-1)
    solved = jax.scipy.linalg.solve_triangular(system, stacked, lower=True, unit_diagonal=True)
    value_width = values.shape[-1]
    update_value = solved[..., :value_width]
    update_key = solved[..., value_width:]
    query_dots = jnp.einsum('...td,...sd->...ts', queries, key_rows, precision=highest)
    attend = jnp.where(causal, query_dots * decay_table, 0.0)
    scaled_query = growth[..., None] * queries
    tail_keys = jnp.exp(cumulative[..., -1:] - cumulative)[..., None] * key_rows
    end_decay = growth[..., -1]
    return (scaled_query, attend, update_value, update_key, tail_keys, end_decay)

def reference(hidden_states, proj_ba, query_in, key_in, value_in, conv_query, conv_key, convolution_value_taps, decay_scale, dt_bias):
    logits = jnp.dot(hidden_states.astype(jnp.float32), proj_ba.astype(jnp.float32), preferred_element_type=jnp.float32)
    log_decay = -decay_scale[None, :] * jax.nn.softplus(logits[:, 0::2] + dt_bias[None, :])
    write_rate = jax.nn.sigmoid(logits[:, 1::2])
    group_size = HV // HK
    block_count = TOKENS // BLOCK
    query_scale = 1.0 / math.sqrt(DK)

    def one_head(head_index):
        key_start = head_index // group_size * DK
        value_start = head_index * DV
        query_cols = lax.dynamic_slice_in_dim(query_in, key_start, DK, 1)
        key_cols = lax.dynamic_slice_in_dim(key_in, key_start, DK, 1)
        value_cols = lax.dynamic_slice_in_dim(value_in, value_start, DV, 1)
        query_taps = lax.dynamic_slice_in_dim(conv_query, key_start, DK, 1)
        key_taps = lax.dynamic_slice_in_dim(conv_key, key_start, DK, 1)
        value_taps = lax.dynamic_slice_in_dim(convolution_value_taps, value_start, DV, 1)
        unit_query = unit_norm(causal_conv(query_cols, query_taps), query_scale)
        unit_keys = unit_norm(causal_conv(key_cols, key_taps), 1.0)
        mixed_values = causal_conv(value_cols, value_taps)
        decay_col = lax.dynamic_slice_in_dim(log_decay, head_index, 1, 1)[:, 0]
        rate_col = lax.dynamic_slice_in_dim(write_rate, head_index, 1, 1)[:, 0]
        pieces = block_terms(unit_query.reshape(block_count, BLOCK, DK), unit_keys.reshape(block_count, BLOCK, DK), mixed_values.reshape(block_count, BLOCK, DV), decay_col.reshape(block_count, BLOCK), rate_col.reshape(block_count, BLOCK))

        def block_step(state_now, piece_set):
            query_part, attend_part, value_part, key_part, tail_part, end_part = piece_set
            errors = value_part - jnp.dot(key_part, state_now, precision=highest)
            produced = jnp.dot(query_part, state_now, precision=highest) + jnp.dot(attend_part, errors, precision=highest)
            next_state = end_part * state_now + jnp.dot(tail_part.T, errors, precision=highest)
            return (next_state, produced)
        initial = jnp.zeros((DK, DV), jnp.float32)
        unused, produced = lax.scan(block_step, initial, pieces)
        return produced.reshape(TOKENS, DV)
    stacked = lax.map(one_head, jnp.arange(HV, dtype=jnp.int32))
    return jnp.transpose(stacked, (1, 0, 2)).reshape(TOKENS, HV * DV)
```

```python
import functools
import math

import jax
import jax.numpy as jnp
from jax import lax
from jax.experimental import pallas as pl
from jax.experimental.pallas import tpu as pltpu
from jax.sharding import PartitionSpec as P

DK = 128
DV = 128
KCONV = 4
C = 128
ZROW = 8
GROUP = 4
HALO = 16

MESH = pl.DeviceIdType.MESH
F32 = jnp.float32
BF16 = jnp.bfloat16


def split(a):
    hi = a.astype(BF16)
    return hi, (a - hi.astype(F32)).astype(BF16)


def mm(a, b, dims=(((1,), (0,)), ((), ()))):
    dot = functools.partial(lax.dot_general, dimension_numbers=dims, preferred_element_type=F32)
    return dot(a[0], b[0]) + (dot(a[0], b[1]) + dot(a[1], b[0]))


NT = (((1,), (1,)), ((), ()))


def iota(shape, axis):
    return lax.broadcasted_iota(jnp.int32, shape, axis)


def silu(u):
    return u / (1.0 + jnp.exp(-u))


def exchange_kernel(heads, hid, proj, q, k, v, g_out, halo_out, part, parts, tail, halo,
                    send, recv, hsend, hrecv):
    seq, head = lax.axis_index("seq"), lax.axis_index("head")
    shards = lax.axis_size("seq")
    after, before = lax.rem(seq + 1, shards), lax.rem(seq + shards - 1, shards)
    barrier = pltpu.get_barrier_semaphore()
    for o in range(1, heads):
        pl.semaphore_signal(barrier, inc=1, device_id={"head": lax.rem(head + o, heads)}, device_id_type=MESH)
    for s in (after, before):
        pl.semaphore_signal(barrier, inc=1, device_id={"seq": s}, device_id_type=MESH)

    rows = q.shape[0]
    wq, wk = q.shape[1], k.shape[1]
    tail[:, :wq] = q[rows - HALO:, :]
    tail[:, wq:wq + wk] = k[rows - HALO:, :]
    tail[:, wq + wk:] = v[rows - HALO:, :]
    logits = jnp.dot(hid[...], proj[...], preferred_element_type=F32)
    flat = jnp.transpose(logits)
    per = flat.shape[0] // heads
    for p in range(heads):
        part[p] = flat[p * per:(p + 1) * per, :]
    pl.semaphore_wait(barrier, heads + 1)

    hcopy = pltpu.make_async_remote_copy(
        src_ref=tail, dst_ref=halo, send_sem=hsend, recv_sem=hrecv,
        device_id={"seq": after}, device_id_type=MESH)
    hcopy.start()
    copies = []
    for o in range(1, heads):
        to = lax.rem(head + o, heads)
        copy = pltpu.make_async_remote_copy(
            src_ref=part.at[to], dst_ref=parts.at[o - 1], send_sem=send.at[o - 1], recv_sem=recv.at[o - 1],
            device_id={"head": to}, device_id_type=MESH)
        copy.start()
        copies.append(copy)
    total = part[head]
    for o, copy in enumerate(copies):
        copy.wait_recv()
        total = total + parts[o]
    g_out[...] = total
    hcopy.wait_recv()
    halo_out[...] = jnp.where(seq == 0, 0.0, halo[...].astype(F32)).astype(BF16)
    hcopy.wait_send()
    for copy in copies:
        copy.wait_send()


def exchange(hid, proj, q, k, v, heads):
    rows = hid.shape[0]
    per = proj.shape[1] // heads
    width = q.shape[1] + k.shape[1] + v.shape[1]
    vm = pl.BlockSpec(memory_space=pltpu.VMEM)
    return pl.pallas_call(
        functools.partial(exchange_kernel, heads),
        out_shape=(jax.ShapeDtypeStruct((per, rows), F32), jax.ShapeDtypeStruct((HALO, width), BF16)),
        in_specs=[vm] * 5,
        out_specs=(vm, vm),
        scratch_shapes=[
            pltpu.VMEM((heads, per, rows), F32),
            pltpu.VMEM((heads - 1, per, rows), F32),
            pltpu.VMEM((HALO, width), BF16),
            pltpu.VMEM((HALO, width), BF16),
            pltpu.SemaphoreType.DMA((heads - 1,)),
            pltpu.SemaphoreType.DMA((heads - 1,)),
            pltpu.SemaphoreType.DMA,
            pltpu.SemaphoreType.DMA,
        ],
        compiler_params=pltpu.CompilerParams(collective_id=0, has_side_effects=True),
        name="exchange",
    )(hid, proj, q, k, v)


def inverse(a, r, c):
    t = jnp.where(r == c, 1.0, 0.0) - jnp.where((r >> 1) == (c >> 1), a, 0.0)
    for level in range(1, 7):
        off = ((r >> (level + 1)) == (c >> (level + 1))) & ((r >> level) != (c >> level))
        ts = split(t)
        t = t - mm(ts, split(mm(split(jnp.where(off, a, 0.0)), ts)))
    return t


def local_kernel(heads, group, scale_ref, bias_ref, g, q, k, v, cq, ck, cv, halo,
                 r_out, o_out, ms_out, pad, state):
    step = pl.program_id(0)
    wq, wk = q.shape[1], k.shape[1]
    width = pad.shape[1]

    @pl.when(step == 0)
    def _():
        pad[0:8, :] = halo[HALO - 8:HALO, :].astype(F32)
        eye = jnp.where(iota((DK, DK), 0) == iota((DK, DK), 1), 1.0, 0.0)
        for h in range(heads):
            state[h, 0] = eye
            state[h, 1] = jnp.zeros((DK, DV), F32)

    @pl.when(step > 0)
    def _():
        pad[0:8, :] = pad[C:C + 8, :]

    pad[8:8 + C, :wq] = q[...].astype(F32)
    pad[8:8 + C, wq:wq + wk] = k[...].astype(F32)
    pad[8:8 + C, wq + wk:] = v[...].astype(F32)

    def conv(col, taps, tcol):
        total = None
        for j in range(KCONV):
            term = taps[j:j + 1, tcol:tcol + DK].astype(F32) * pad[5 + j:5 + j + C, col:col + DK]
            total = term if total is None else total + term
        return silu(total)

    def unit(u, factor):
        return u * (lax.rsqrt(jnp.sum(u * u, axis=-1, keepdims=True) + 1e-06) * factor)

    r, c = iota((C, C), 0), iota((C, C), 1)
    causal, strict = r >= c, r > c

    decays, rates = [], []
    for h in range(heads):
        u = g[2 * h:2 * h + 1, :] + bias_ref[h]
        e = jnp.exp(-jnp.abs(u))
        w = 1.0 + e
        log1p = jnp.where(w == 1.0, e, jnp.log(w) * (e / jnp.where(w == 1.0, 1.0, w - 1.0)))
        decays.append(-scale_ref[h] * (jnp.maximum(u, 0.0) + log1p))
        rates.append(1.0 / (1.0 + jnp.exp(-g[2 * h + 1:2 * h + 2, :])))
    ones = jnp.where(r <= c, 1.0, 0.0)
    table = jnp.concatenate(decays + rates, axis=0)
    cum = lax.dot_general(table, ones, (((1,), (0,)), ((), ())), precision=lax.Precision.HIGHEST,
                          preferred_element_type=F32)
    cum_col, rate_col = jnp.transpose(cum), jnp.transpose(table)

    for n in range(heads // group):
        queries = unit(conv(n * DK, cq, n * DK), 1.0 / math.sqrt(DK))
        keys = unit(conv(wq + n * DK, ck, n * DK), 1.0)
        keys_s = split(keys)
        queries_s = split(queries)
        kk = mm(keys_s, keys_s, NT)
        qk = mm(queries_s, keys_s, NT)
        keys_t = jnp.transpose(keys)
        for h in range(n * group, (n + 1) * group):
            values = conv(wq + wk + h * DV, cv, h * DV)
            gc, gr = cum_col[:, h:h + 1], cum[h:h + 1, :]
            beta = rate_col[:, heads + h:heads + h + 1]
            decay = jnp.where(causal, jnp.exp(jnp.where(causal, gc - gr, 0.0)), 0.0)
            solve = inverse(jnp.where(strict, beta * decay * kk, 0.0), r, c)
            growth = jnp.exp(gc)
            solve_s = split(solve)
            wu = mm(solve_s, split(jnp.concatenate([(beta * growth) * keys, beta * values], axis=1)))
            x = jnp.concatenate([state[h, 0], state[h, 1]], axis=1)
            x_s = split(x)
            y = mm(split(-wu[:, :DK]), x_s)
            y = jnp.concatenate([y[:, :DK], y[:, DK:] + wu[:, DK:]], axis=1)
            y_s = split(y)
            out = mm(split(growth * queries), x_s) + mm(split(decay * qk), y_s)
            r_out[:, h * DK:(h + 1) * DK] = out[:, :DK]
            o_out[:, h * DV:(h + 1) * DV] = out[:, DK:]
            last = cum[h:h + 1, C - 1:C]
            x = jnp.exp(last) * x + mm(split(keys_t * jnp.exp(last - gr)), y_s)
            state[h, 0] = x[:, :DK]
            state[h, 1] = x[:, DK:]

    ms_out[...] = state[...]


def local(scale, bias, g, q, k, v, cq, ck, cv, halo):
    heads = scale.shape[0]
    rows = q.shape[0]
    group = heads // (q.shape[1] // DK)
    smem = pl.BlockSpec(memory_space=pltpu.SMEM)

    def rowblock(a):
        return pl.BlockSpec((C, a.shape[1]), lambda i: (i, 0))

    def whole(a):
        return pl.BlockSpec(a.shape, lambda i: (0,) * a.ndim)

    width = q.shape[1] + k.shape[1] + v.shape[1]
    return pl.pallas_call(
        functools.partial(local_kernel, heads, group),
        grid=(rows // C,),
        out_shape=(
            jax.ShapeDtypeStruct((rows, heads * DK), F32),
            jax.ShapeDtypeStruct((rows, heads * DV), F32),
            jax.ShapeDtypeStruct((heads, 2, DK, DV), F32),
        ),
        in_specs=[smem, smem, pl.BlockSpec((g.shape[0], C), lambda i: (0, i)), rowblock(q), rowblock(k),
                  rowblock(v), whole(cq), whole(ck), whole(cv), whole(halo)],
        out_specs=(
            pl.BlockSpec((C, heads * DK), lambda i: (i, 0)),
            pl.BlockSpec((C, heads * DV), lambda i: (i, 0)),
            pl.BlockSpec((heads, 2, DK, DV), lambda i: (0, 0, 0, 0)),
        ),
        scratch_shapes=[pltpu.VMEM((C + 8, width), F32), pltpu.VMEM((heads, 2, DK, DV), F32)],
        compiler_params=pltpu.CompilerParams(dimension_semantics=("arbitrary",)),
        name="local",
    )(scale, bias, g, q, k, v, cq, ck, cv, halo)


def wide(ref, *at):
    return jnp.concatenate([ref[(*at, 0)], ref[(*at, 1)]], axis=1)


def then(later_move, later_state, x):
    y = mm(split(later_move), split(x))
    return y[:, :DK], y[:, DK:] + later_state


def scan_kernel(rows_x, ms, e_out, gathered, prefix, mine, other, total, rows, entry, staged, arrived,
                send1, recv1, send2, recv2, send3, recv3, send4, recv4):
    seq = lax.axis_index("seq")
    z = lax.rem(seq, ZROW)
    x = seq // ZROW
    half = z // GROUP
    place = lax.rem(z, GROUP)
    own = jnp.where(half == 0, place, GROUP - 1 - place)
    base = seq - place
    mirror = x * ZROW + (ZROW - 1 - z)

    def owned(p):
        return jnp.where(half == 0, p, GROUP - 1 - p)

    barrier = pltpu.get_barrier_semaphore()
    for o in range(1, GROUP):
        pl.semaphore_signal(barrier, inc=1, device_id={"seq": base + lax.rem(place + o, GROUP)}, device_id_type=MESH)
    pl.semaphore_signal(barrier, inc=1, device_id={"seq": mirror}, device_id_type=MESH)
    for o in range(1, rows_x):
        pl.semaphore_signal(barrier, inc=1, device_id={"seq": lax.rem(x + o, rows_x) * ZROW + z}, device_id_type=MESH)
    pl.semaphore_wait(barrier, GROUP - 1 + 1 + rows_x - 1)

    first = []
    for o in range(1, GROUP):
        p = lax.rem(place + o, GROUP)
        copy = pltpu.make_async_remote_copy(
            src_ref=ms.at[owned(p)], dst_ref=gathered.at[place], send_sem=send1.at[o - 1],
            recv_sem=recv1.at[place], device_id={"seq": base + p}, device_id_type=MESH)
        copy.start()
        first.append(copy)
    gathered[place] = ms[own]
    def arrive(t):
        @pl.when(place != t)
        def _():
            pltpu.make_async_remote_copy(
                src_ref=ms.at[0], dst_ref=gathered.at[t], send_sem=send1.at[0], recv_sem=recv1.at[t],
                device_id={"seq": mirror}, device_id_type=MESH).wait_recv()

    arrive(0)
    prefix[1] = gathered[0]
    for t in range(1, GROUP):
        arrive(t)
        move, state = then(gathered[t, 0], gathered[t, 1], wide(prefix, t))
        if t < GROUP - 1:
            prefix[t + 1, 0], prefix[t + 1, 1] = move, state
        else:
            mine[0], mine[1] = move, state

    second = pltpu.make_async_remote_copy(
        src_ref=mine, dst_ref=other, send_sem=send2, recv_sem=recv2,
        device_id={"seq": mirror}, device_id_type=MESH)
    second.start()
    second.wait_recv()
    early = half == 0
    a_move, a_state = jnp.where(early, mine[0], other[0]), jnp.where(early, mine[1], other[1])
    b_move, b_state = jnp.where(early, other[0], mine[0]), jnp.where(early, other[1], mine[1])
    total[0], total[1] = then(b_move, b_state, jnp.concatenate([a_move, a_state], axis=1))

    def to_row(d):
        return pltpu.make_async_remote_copy(
            src_ref=total, dst_ref=rows.at[x], send_sem=send3.at[d], recv_sem=recv3.at[x],
            device_id={"seq": d * ZROW + z}, device_id_type=MESH)

    for d in range(1, rows_x):
        @pl.when(x < d)
        def _(d=d):
            to_row(d).start()
    entry[...] = jnp.zeros_like(entry)
    for t in range(rows_x - 1):
        @pl.when(t < x)
        def _(t=t):
            pltpu.make_async_remote_copy(
                src_ref=total, dst_ref=rows.at[t], send_sem=send3.at[0], recv_sem=recv3.at[t],
                device_id={"seq": mirror}, device_id_type=MESH).wait_recv()
            if t == 0:
                entry[...] = rows[0, 1]
            else:
                entry[...] = mm(split(rows[t, 0]), split(entry[...])) + rows[t, 1]
    for d in range(1, rows_x):
        @pl.when(x < d)
        def _(d=d):
            to_row(d).wait_send()

    e = entry[...]
    e = jnp.where(early, e, mm(split(a_move), split(e)) + a_state)
    e_s = split(e)
    staged[0] = e
    for t in range(1, GROUP):
        staged[t] = mm(split(prefix[t, 0]), e_s) + prefix[t, 1]
    last = []
    for o in range(1, GROUP):
        p = lax.rem(place + o, GROUP)
        copy = pltpu.make_async_remote_copy(
            src_ref=staged.at[p], dst_ref=arrived.at[own], send_sem=send4.at[o - 1], recv_sem=recv4.at[own],
            device_id={"seq": base + p}, device_id_type=MESH)
        copy.start()
        last.append(copy)
    arrived[own] = staged[place]
    for h in range(GROUP):
        @pl.when(own != h)
        def _(h=h):
            pltpu.make_async_remote_copy(
                src_ref=staged.at[0], dst_ref=arrived.at[h], send_sem=send4.at[0], recv_sem=recv4.at[h],
                device_id={"seq": mirror}, device_id_type=MESH).wait_recv()
    e_out[...] = arrived[...]
    for copy in first + [second] + last:
        copy.wait_send()


def entering(ms, shards):
    heads = ms.shape[0]
    rows_x = shards // ZROW
    assert heads == GROUP
    vm = pl.BlockSpec(memory_space=pltpu.VMEM)
    dma = pltpu.SemaphoreType.DMA
    pair = (2, DK, DV)
    return pl.pallas_call(
        functools.partial(scan_kernel, rows_x),
        out_shape=jax.ShapeDtypeStruct((heads, DK, DV), F32),
        in_specs=[vm],
        out_specs=vm,
        scratch_shapes=[
            pltpu.VMEM((GROUP, *pair), F32),
            pltpu.VMEM((GROUP, *pair), F32),
            pltpu.VMEM(pair, F32),
            pltpu.VMEM(pair, F32),
            pltpu.VMEM(pair, F32),
            pltpu.VMEM((rows_x, *pair), F32),
            pltpu.VMEM((DK, DV), F32),
            pltpu.VMEM((GROUP, DK, DV), F32),
            pltpu.VMEM((GROUP, DK, DV), F32),
            dma((GROUP - 1,)), dma((GROUP,)),
            dma, dma,
            dma((rows_x,)), dma((rows_x,)),
            dma((GROUP - 1,)), dma((GROUP,)),
        ],
        compiler_params=pltpu.CompilerParams(collective_id=1, has_side_effects=True),
        name="entering",
    )(ms)


def final_kernel(heads, r, o, e, out):
    for h in range(heads):
        cols = slice(h * DK, (h + 1) * DK)
        out[:, cols] = o[:, cols] + mm(split(r[:, cols]), split(e[h]))


def final(r, o, e):
    rows, width = r.shape
    spec = pl.BlockSpec((C, width), lambda i: (i, 0))
    return pl.pallas_call(
        functools.partial(final_kernel, e.shape[0]),
        grid=(rows // C,),
        out_shape=jax.ShapeDtypeStruct(o.shape, F32),
        in_specs=[spec, spec, pl.BlockSpec(e.shape, lambda i: (0, 0, 0))],
        out_specs=spec,
        compiler_params=pltpu.CompilerParams(dimension_semantics=("arbitrary",)),
        name="final",
    )(r, o, e)


def solution(mesh):
    heads, shards = mesh.shape["head"], mesh.shape["seq"]

    def per_device(hid, proj, q, k, v, cq, ck, cv, scale, bias):
        g, halo = exchange(hid, proj, q, k, v, heads)
        r, o, ms = local(scale, bias, g, q, k, v, cq, ck, cv, halo)
        return final(r, o, entering(ms, shards))

    placed = (
        P("seq", "head"), P("head", None), P("seq", "head"), P("seq", "head"), P("seq", "head"),
        P(None, "head"), P(None, "head"), P(None, "head"), P("head"), P("head"),
    )
    return jax.shard_map(per_device, mesh=mesh, in_specs=placed, out_specs=P("seq", "head"), check_vma=False)
```

```python
import functools
import math

import jax
import jax.numpy as jnp
from jax import lax
from jax.experimental import pallas as pl
from jax.experimental.pallas import tpu as pltpu
from jax.sharding import PartitionSpec as P

DK = 128
DV = 128
KCONV = 4
C = 128
ZROW = 8
GROUP = 4
HALO = 16

MESH = pl.DeviceIdType.MESH
F32 = jnp.float32
BF16 = jnp.bfloat16


def split(a):
    hi = a.astype(BF16)
    return hi, (a - hi.astype(F32)).astype(BF16)


def mm(a, b, dims=(((1,), (0,)), ((), ()))):
    dot = functools.partial(lax.dot_general, dimension_numbers=dims, preferred_element_type=F32)
    return dot(a[0], b[0]) + (dot(a[0], b[1]) + dot(a[1], b[0]))


NT = (((1,), (1,)), ((), ()))


def iota(shape, axis):
    return lax.broadcasted_iota(jnp.int32, shape, axis)


def silu(u):
    return u / (1.0 + jnp.exp(-u))


def exchange_kernel(heads, hid, proj, q, k, v, g_out, halo_out, part, parts, tail, halo,
                    send, recv, hsend, hrecv):
    seq, head = lax.axis_index("seq"), lax.axis_index("head")
    shards = lax.axis_size("seq")
    after, before = lax.rem(seq + 1, shards), lax.rem(seq + shards - 1, shards)
    barrier = pltpu.get_barrier_semaphore()
    for o in range(1, heads):
        pl.semaphore_signal(barrier, inc=1, device_id={"head": lax.rem(head + o, heads)}, device_id_type=MESH)
    for s in (after, before):
        pl.semaphore_signal(barrier, inc=1, device_id={"seq": s}, device_id_type=MESH)

    rows = q.shape[0]
    wq, wk = q.shape[1], k.shape[1]
    tail[:, :wq] = q[rows - HALO:, :]
    tail[:, wq:wq + wk] = k[rows - HALO:, :]
    tail[:, wq + wk:] = v[rows - HALO:, :]
    logits = jnp.dot(hid[...], proj[...], preferred_element_type=F32)
    flat = jnp.transpose(logits)
    per = flat.shape[0] // heads
    for p in range(heads):
        part[p] = flat[p * per:(p + 1) * per, :]
    pl.semaphore_wait(barrier, heads + 1)

    hcopy = pltpu.make_async_remote_copy(
        src_ref=tail, dst_ref=halo, send_sem=hsend, recv_sem=hrecv,
        device_id={"seq": after}, device_id_type=MESH)
    hcopy.start()
    copies = []
    for o in range(1, heads):
        to = lax.rem(head + o, heads)
        copy = pltpu.make_async_remote_copy(
            src_ref=part.at[to], dst_ref=parts.at[o - 1], send_sem=send.at[o - 1], recv_sem=recv.at[o - 1],
            device_id={"head": to}, device_id_type=MESH)
        copy.start()
        copies.append(copy)
    total = part[head]
    for o, copy in enumerate(copies):
        copy.wait_recv()
        total = total + parts[o]
    g_out[...] = total
    hcopy.wait_recv()
    halo_out[...] = jnp.where(seq == 0, 0.0, halo[...].astype(F32)).astype(BF16)
    hcopy.wait_send()
    for copy in copies:
        copy.wait_send()


def exchange(hid, proj, q, k, v, heads):
    rows = hid.shape[0]
    per = proj.shape[1] // heads
    width = q.shape[1] + k.shape[1] + v.shape[1]
    vm = pl.BlockSpec(memory_space=pltpu.VMEM)
    return pl.pallas_call(
        functools.partial(exchange_kernel, heads),
        out_shape=(jax.ShapeDtypeStruct((per, rows), F32), jax.ShapeDtypeStruct((HALO, width), BF16)),
        in_specs=[vm] * 5,
        out_specs=(vm, vm),
        scratch_shapes=[
            pltpu.VMEM((heads, per, rows), F32),
            pltpu.VMEM((heads - 1, per, rows), F32),
            pltpu.VMEM((HALO, width), BF16),
            pltpu.VMEM((HALO, width), BF16),
            pltpu.SemaphoreType.DMA((heads - 1,)),
            pltpu.SemaphoreType.DMA((heads - 1,)),
            pltpu.SemaphoreType.DMA,
            pltpu.SemaphoreType.DMA,
        ],
        compiler_params=pltpu.CompilerParams(collective_id=0, has_side_effects=True),
        name="exchange",
    )(hid, proj, q, k, v)


def inverses(systems, r, c):
    lane, sub = iota((8, C), 1), iota((8, C), 0)
    group = lane >> 3
    solved = []
    for a in systems:
        packed = a[0:8, :]
        for j in range(1, C // 8):
            packed = jnp.where(group == j, a[8 * j:8 * j + 8, :], packed)
        t = jnp.where((lane & 7) == sub, 1.0, 0.0)
        for m in range(7):
            factor = jnp.take_along_axis(packed, (lane & ~7) + m, axis=1)
            t = t - factor * t[m:m + 1, :]
        solved.append(jnp.concatenate([jnp.where(group == j, t, 0.0) for j in range(C // 8)], axis=0))
    for level in range(3, 7):
        off = ((r >> (level + 1)) == (c >> (level + 1))) & ((r >> level) != (c >> level))
        parts = [split(t) for t in solved]
        inner = [mm(split(jnp.where(off, a, 0.0)), ts) for a, ts in zip(systems, parts)]
        solved = [t - mm(ts, split(p)) for t, ts, p in zip(solved, parts, inner)]
    return solved


def local_kernel(heads, group, scale_ref, bias_ref, g, q, k, v, cq, ck, cv, halo,
                 r_out, o_out, ms_out, pad, state):
    step = pl.program_id(0)
    wq, wk = q.shape[1], k.shape[1]
    width = pad.shape[1]

    @pl.when(step == 0)
    def _():
        pad[0:8, :] = halo[HALO - 8:HALO, :].astype(F32)
        eye = jnp.where(iota((DK, DK), 0) == iota((DK, DK), 1), 1.0, 0.0)
        for h in range(heads):
            state[h, 0] = eye
            state[h, 1] = jnp.zeros((DK, DV), F32)

    @pl.when(step > 0)
    def _():
        pad[0:8, :] = pad[C:C + 8, :]

    pad[8:8 + C, :wq] = q[...].astype(F32)
    pad[8:8 + C, wq:wq + wk] = k[...].astype(F32)
    pad[8:8 + C, wq + wk:] = v[...].astype(F32)

    def conv(col, taps, tcol):
        total = None
        for j in range(KCONV):
            term = taps[j:j + 1, tcol:tcol + DK].astype(F32) * pad[5 + j:5 + j + C, col:col + DK]
            total = term if total is None else total + term
        return silu(total)

    def unit(u, factor):
        return u * (lax.rsqrt(jnp.sum(u * u, axis=-1, keepdims=True) + 1e-06) * factor)

    r, c = iota((C, C), 0), iota((C, C), 1)
    causal, strict = r >= c, r > c

    decays, rates = [], []
    for h in range(heads):
        u = g[2 * h:2 * h + 1, :] + bias_ref[h]
        e = jnp.exp(-jnp.abs(u))
        w = 1.0 + e
        log1p = jnp.where(w == 1.0, e, jnp.log(w) * (e / jnp.where(w == 1.0, 1.0, w - 1.0)))
        decays.append(-scale_ref[h] * (jnp.maximum(u, 0.0) + log1p))
        rates.append(1.0 / (1.0 + jnp.exp(-g[2 * h + 1:2 * h + 2, :])))
    ones = jnp.where(r <= c, 1.0, 0.0)
    table = jnp.concatenate(decays + rates, axis=0)
    cum = lax.dot_general(table, ones, (((1,), (0,)), ((), ())), precision=lax.Precision.HIGHEST,
                          preferred_element_type=F32)
    cum_col, rate_col = jnp.transpose(cum), jnp.transpose(table)

    key_heads = range(heads // group)
    queries = [unit(conv(n * DK, cq, n * DK), 1.0 / math.sqrt(DK)) for n in key_heads]
    keys = [unit(conv(wq + n * DK, ck, n * DK), 1.0) for n in key_heads]
    keys_s = [split(x) for x in keys]
    kk = [mm(x, x, NT) for x in keys_s]
    qk = [mm(split(queries[n]), keys_s[n], NT) for n in key_heads]
    keys_t = [jnp.transpose(x) for x in keys]
    every = range(heads)
    betas = [rate_col[:, heads + h:heads + h + 1] for h in every]
    decay = []
    for h in every:
        gap = cum_col[:, h:h + 1] - cum[h:h + 1, :]
        decay.append(jnp.where(causal, jnp.exp(jnp.where(causal, gap, 0.0)), 0.0))
    solved = inverses([jnp.where(strict, betas[h] * decay[h] * kk[h // group], 0.0) for h in every], r, c)
    growth = [jnp.exp(cum_col[:, h:h + 1]) for h in every]
    right = []
    for h in every:
        values = conv(wq + wk + h * DV, cv, h * DV)
        right.append(split(jnp.concatenate([(betas[h] * growth[h]) * keys[h // group], betas[h] * values], axis=1)))
    wu = [mm(split(solved[h]), right[h]) for h in every]
    xs = [jnp.concatenate([state[h, 0], state[h, 1]], axis=1) for h in every]
    xs_s = [split(x) for x in xs]
    ys = [mm(split(-wu[h][:, :DK]), xs_s[h]) for h in every]
    ys_s = [split(jnp.concatenate([ys[h][:, :DK], ys[h][:, DK:] + wu[h][:, DK:]], axis=1)) for h in every]
    for h in every:
        last = cum[h:h + 1, C - 1:C]
        x = jnp.exp(last) * xs[h] + mm(split(keys_t[h // group] * jnp.exp(last - cum[h:h + 1, :])), ys_s[h])
        state[h, 0] = x[:, :DK]
        state[h, 1] = x[:, DK:]
    for h in every:
        out = mm(split(growth[h] * queries[h // group]), xs_s[h]) + mm(split(decay[h] * qk[h // group]), ys_s[h])
        r_out[:, h * DK:(h + 1) * DK] = out[:, :DK]
        o_out[:, h * DV:(h + 1) * DV] = out[:, DK:]

    ms_out[...] = state[...]


def local(scale, bias, g, q, k, v, cq, ck, cv, halo):
    heads = scale.shape[0]
    rows = q.shape[0]
    group = heads // (q.shape[1] // DK)
    smem = pl.BlockSpec(memory_space=pltpu.SMEM)

    def rowblock(a):
        return pl.BlockSpec((C, a.shape[1]), lambda i: (i, 0))

    def whole(a):
        return pl.BlockSpec(a.shape, lambda i: (0,) * a.ndim)

    width = q.shape[1] + k.shape[1] + v.shape[1]
    return pl.pallas_call(
        functools.partial(local_kernel, heads, group),
        grid=(rows // C,),
        out_shape=(
            jax.ShapeDtypeStruct((rows, heads * DK), F32),
            jax.ShapeDtypeStruct((rows, heads * DV), F32),
            jax.ShapeDtypeStruct((heads, 2, DK, DV), F32),
        ),
        in_specs=[smem, smem, pl.BlockSpec((g.shape[0], C), lambda i: (0, i)), rowblock(q), rowblock(k),
                  rowblock(v), whole(cq), whole(ck), whole(cv), whole(halo)],
        out_specs=(
            pl.BlockSpec((C, heads * DK), lambda i: (i, 0)),
            pl.BlockSpec((C, heads * DV), lambda i: (i, 0)),
            pl.BlockSpec((heads, 2, DK, DV), lambda i: (0, 0, 0, 0)),
        ),
        scratch_shapes=[pltpu.VMEM((C + 8, width), F32), pltpu.VMEM((heads, 2, DK, DV), F32)],
        compiler_params=pltpu.CompilerParams(dimension_semantics=("arbitrary",)),
        name="local",
    )(scale, bias, g, q, k, v, cq, ck, cv, halo)


def wide(ref, *at):
    return jnp.concatenate([ref[(*at, 0)], ref[(*at, 1)]], axis=1)


def then(later_move, later_state, x):
    y = mm(split(later_move), split(x))
    return y[:, :DK], y[:, DK:] + later_state


def scan_kernel(rows_x, ms, e_out, gathered, prefix, mine, other, total, rows, entry, staged, arrived,
                send1, recv1, send2, recv2, send3, recv3, send4, recv4):
    seq = lax.axis_index("seq")
    z = lax.rem(seq, ZROW)
    x = seq // ZROW
    half = z // GROUP
    place = lax.rem(z, GROUP)
    own = jnp.where(half == 0, place, GROUP - 1 - place)
    base = seq - place
    mirror = x * ZROW + (ZROW - 1 - z)

    def owned(p):
        return jnp.where(half == 0, p, GROUP - 1 - p)

    barrier = pltpu.get_barrier_semaphore()
    for o in range(1, GROUP):
        pl.semaphore_signal(barrier, inc=1, device_id={"seq": base + lax.rem(place + o, GROUP)}, device_id_type=MESH)
    pl.semaphore_signal(barrier, inc=1, device_id={"seq": mirror}, device_id_type=MESH)
    for o in range(1, rows_x):
        pl.semaphore_signal(barrier, inc=1, device_id={"seq": lax.rem(x + o, rows_x) * ZROW + z}, device_id_type=MESH)
    pl.semaphore_wait(barrier, GROUP - 1 + 1 + rows_x - 1)

    first = []
    for o in range(1, GROUP):
        p = lax.rem(place + o, GROUP)
        copy = pltpu.make_async_remote_copy(
            src_ref=ms.at[owned(p)], dst_ref=gathered.at[place], send_sem=send1.at[o - 1],
            recv_sem=recv1.at[place], device_id={"seq": base + p}, device_id_type=MESH)
        copy.start()
        first.append(copy)
    gathered[place] = ms[own]
    def arrive(t):
        @pl.when(place != t)
        def _():
            pltpu.make_async_remote_copy(
                src_ref=ms.at[0], dst_ref=gathered.at[t], send_sem=send1.at[0], recv_sem=recv1.at[t],
                device_id={"seq": mirror}, device_id_type=MESH).wait_recv()

    arrive(0)
    prefix[1] = gathered[0]
    for t in range(1, GROUP):
        arrive(t)
        move, state = then(gathered[t, 0], gathered[t, 1], wide(prefix, t))
        if t < GROUP - 1:
            prefix[t + 1, 0], prefix[t + 1, 1] = move, state
        else:
            mine[0], mine[1] = move, state

    second = pltpu.make_async_remote_copy(
        src_ref=mine, dst_ref=other, send_sem=send2, recv_sem=recv2,
        device_id={"seq": mirror}, device_id_type=MESH)
    second.start()
    second.wait_recv()
    early = half == 0
    a_move, a_state = jnp.where(early, mine[0], other[0]), jnp.where(early, mine[1], other[1])
    b_move, b_state = jnp.where(early, other[0], mine[0]), jnp.where(early, other[1], mine[1])
    total[0], total[1] = then(b_move, b_state, jnp.concatenate([a_move, a_state], axis=1))

    def to_row(d):
        return pltpu.make_async_remote_copy(
            src_ref=total, dst_ref=rows.at[x], send_sem=send3.at[d], recv_sem=recv3.at[x],
            device_id={"seq": d * ZROW + z}, device_id_type=MESH)

    for d in range(1, rows_x):
        @pl.when(x < d)
        def _(d=d):
            to_row(d).start()
    entry[...] = jnp.zeros_like(entry)
    for t in range(rows_x - 1):
        @pl.when(t < x)
        def _(t=t):
            pltpu.make_async_remote_copy(
                src_ref=total, dst_ref=rows.at[t], send_sem=send3.at[0], recv_sem=recv3.at[t],
                device_id={"seq": mirror}, device_id_type=MESH).wait_recv()
            if t == 0:
                entry[...] = rows[0, 1]
            else:
                entry[...] = mm(split(rows[t, 0]), split(entry[...])) + rows[t, 1]
    for d in range(1, rows_x):
        @pl.when(x < d)
        def _(d=d):
            to_row(d).wait_send()

    e = entry[...]
    e = jnp.where(early, e, mm(split(a_move), split(e)) + a_state)
    e_s = split(e)
    staged[0] = e
    for t in range(1, GROUP):
        staged[t] = mm(split(prefix[t, 0]), e_s) + prefix[t, 1]
    last = []
    for o in range(1, GROUP):
        p = lax.rem(place + o, GROUP)
        copy = pltpu.make_async_remote_copy(
            src_ref=staged.at[p], dst_ref=arrived.at[own], send_sem=send4.at[o - 1], recv_sem=recv4.at[own],
            device_id={"seq": base + p}, device_id_type=MESH)
        copy.start()
        last.append(copy)
    arrived[own] = staged[place]
    for h in range(GROUP):
        @pl.when(own != h)
        def _(h=h):
            pltpu.make_async_remote_copy(
                src_ref=staged.at[0], dst_ref=arrived.at[h], send_sem=send4.at[0], recv_sem=recv4.at[h],
                device_id={"seq": mirror}, device_id_type=MESH).wait_recv()
    e_out[...] = arrived[...]
    for copy in first + [second] + last:
        copy.wait_send()


def entering(ms, shards):
    heads = ms.shape[0]
    rows_x = shards // ZROW
    assert heads == GROUP
    vm = pl.BlockSpec(memory_space=pltpu.VMEM)
    dma = pltpu.SemaphoreType.DMA
    pair = (2, DK, DV)
    return pl.pallas_call(
        functools.partial(scan_kernel, rows_x),
        out_shape=jax.ShapeDtypeStruct((heads, DK, DV), F32),
        in_specs=[vm],
        out_specs=vm,
        scratch_shapes=[
            pltpu.VMEM((GROUP, *pair), F32),
            pltpu.VMEM((GROUP, *pair), F32),
            pltpu.VMEM(pair, F32),
            pltpu.VMEM(pair, F32),
            pltpu.VMEM(pair, F32),
            pltpu.VMEM((rows_x, *pair), F32),
            pltpu.VMEM((DK, DV), F32),
            pltpu.VMEM((GROUP, DK, DV), F32),
            pltpu.VMEM((GROUP, DK, DV), F32),
            dma((GROUP - 1,)), dma((GROUP,)),
            dma, dma,
            dma((rows_x,)), dma((rows_x,)),
            dma((GROUP - 1,)), dma((GROUP,)),
        ],
        compiler_params=pltpu.CompilerParams(collective_id=1, has_side_effects=True),
        name="entering",
    )(ms)


def final_kernel(heads, r, o, e, out):
    for h in range(heads):
        cols = slice(h * DK, (h + 1) * DK)
        out[:, cols] = o[:, cols] + mm(split(r[:, cols]), split(e[h]))


def final(r, o, e):
    rows, width = r.shape
    spec = pl.BlockSpec((C, width), lambda i: (i, 0))
    return pl.pallas_call(
        functools.partial(final_kernel, e.shape[0]),
        grid=(rows // C,),
        out_shape=jax.ShapeDtypeStruct(o.shape, F32),
        in_specs=[spec, spec, pl.BlockSpec(e.shape, lambda i: (0, 0, 0))],
        out_specs=spec,
        compiler_params=pltpu.CompilerParams(dimension_semantics=("arbitrary",)),
        name="final",
    )(r, o, e)


def solution(mesh):
    heads, shards = mesh.shape["head"], mesh.shape["seq"]

    def per_device(hid, proj, q, k, v, cq, ck, cv, scale, bias):
        g, halo = exchange(hid, proj, q, k, v, heads)
        r, o, ms = local(scale, bias, g, q, k, v, cq, ck, cv, halo)
        return final(r, o, entering(ms, shards))

    placed = (
        P("seq", "head"), P("head", None), P("seq", "head"), P("seq", "head"), P("seq", "head"),
        P(None, "head"), P(None, "head"), P(None, "head"), P("head"), P("head"),
    )
    return jax.shard_map(per_device, mesh=mesh, in_specs=placed, out_specs=P("seq", "head"), check_vma=False)
```

```python
import functools
import math

import jax
import jax.numpy as jnp
from jax import lax
from jax.experimental import pallas as pl
from jax.experimental.pallas import tpu as pltpu
from jax.sharding import PartitionSpec as P

DK = 128
DV = 128
KCONV = 4
C = 128
ZROW = 8
GROUP = 4
HALO = 16

MESH = pl.DeviceIdType.MESH
F32 = jnp.float32
BF16 = jnp.bfloat16


def split(a):
    hi = a.astype(BF16)
    return hi, (a - hi.astype(F32)).astype(BF16)


NN = (((1,), (0,)), ((), ()))
NT = (((1,), (1,)), ((), ()))


def mm(a, b, dims=NN):
    dot = functools.partial(lax.dot_general, dimension_numbers=dims, preferred_element_type=F32)
    if dims is NN and a[0].shape[1] == 128:
        pair = jnp.concatenate(a, axis=1)
        hi, lo = (jnp.concatenate([x, x], axis=0) for x in b)
        return dot(pair, hi) + dot(pair, lo)
    return dot(a[0], b[0]) + (dot(a[0], b[1]) + dot(a[1], b[0]))


def iota(shape, axis):
    return lax.broadcasted_iota(jnp.int32, shape, axis)


def silu(u):
    return u / (1.0 + jnp.exp(-u))


def inverses(systems, r, c):
    lane, sub = iota((8, C), 1), iota((8, C), 0)
    group = lane >> 3
    solved = []
    for a in systems:
        packed = a[0:8, :]
        for j in range(1, C // 8):
            packed = jnp.where(group == j, a[8 * j:8 * j + 8, :], packed)
        t = jnp.where((lane & 7) == sub, 1.0, 0.0)
        for m in range(7):
            factor = jnp.take_along_axis(packed, (lane & ~7) + m, axis=1)
            t = t - factor * t[m:m + 1, :]
        solved.append(jnp.concatenate([jnp.where(group == j, t, 0.0) for j in range(C // 8)], axis=0))
    for level in range(3, 7):
        off = ((r >> (level + 1)) == (c >> (level + 1))) & ((r >> level) != (c >> level))
        parts = [split(t) for t in solved]
        inner = [mm(split(jnp.where(off, a, 0.0)), ts) for a, ts in zip(systems, parts)]
        solved = [t - mm(ts, split(p)) for t, ts, p in zip(solved, parts, inner)]
    return solved


def wide(ref, *at):
    return jnp.concatenate([ref[(*at, 0)], ref[(*at, 1)]], axis=1)


def then(later_move, later_state, x):
    y = mm(split(later_move), split(x))
    return y[:, :DK], y[:, DK:] + later_state


SEAT = (0, 3, 1, 2)


def owned_at(p):
    return jnp.where(p == 0, 0, jnp.where(p == GROUP - 1, 1, p + 1))


def whole_kernel(peers, heads, rows_x, scale, bias, hid, proj, q, k, v, cq, ck, cv, out,
                 part, parts, halo, pad, uq, uk, uv, kk, qk, attend, wu, xs, ms, rhi, rlo,
                 gathered, prefix, mine, other, total, tin, ein, entry, enext, full, staged, arrived,
                 send, recv, hsend, hrecv, send1, recv1, send2, recv2, send3, recv3, send4, recv4):
    seq, head = lax.axis_index("seq"), lax.axis_index("head")
    shards = rows_x * ZROW
    z, x = lax.rem(seq, ZROW), seq // ZROW
    half, place = z // GROUP, lax.rem(z, GROUP)
    first_half = half == 0
    base = seq - place
    mirror = x * ZROW + (ZROW - 1 - z)
    after, before = lax.rem(seq + 1, shards), lax.rem(seq + shards - 1, shards)
    own = owned_at(jnp.where(first_half, place, GROUP - 1 - place))
    seats = [jnp.where(first_half, SEAT[h], GROUP - 1 - SEAT[h]) for h in range(heads)]
    rows, wq, wk = q.shape[0], q.shape[1], k.shape[1]
    blocks, key_heads = rows // C, wq // DK
    group = heads // key_heads
    shared = functools.partial(pltpu.make_async_remote_copy, device_id_type=MESH)

    barrier = pltpu.get_barrier_semaphore()
    for o in range(1, peers):
        pl.semaphore_signal(barrier, inc=1, device_id={"head": lax.rem(head + o, peers)}, device_id_type=MESH)
    others = [after, before, mirror]
    others += [base + lax.rem(place + o, GROUP) for o in range(1, GROUP)]
    others += [lax.rem(x + o, rows_x) * ZROW + z for o in range(1, rows_x)]
    for s in others:
        pl.semaphore_signal(barrier, inc=1, device_id={"seq": s}, device_id_type=MESH)

    flat = lax.dot_general(proj[...], hid[...], NT, preferred_element_type=F32)
    per = flat.shape[0] // peers
    for p in range(peers):
        part[p] = flat[p * per:(p + 1) * per, :]
    pl.semaphore_wait(barrier, peers - 1 + len(others))
    copies = []
    for o in range(1, peers):
        to = lax.rem(head + o, peers)
        copies.append(shared(src_ref=part.at[to], dst_ref=parts.at[o - 1], send_sem=send.at[o - 1],
                             recv_sem=recv.at[o - 1], device_id={"head": to}))
    columns = [(q, 0), (k, wq), (v, wq + wk)]
    halos = []
    for i, (src, col) in enumerate(columns):
        halos.append(shared(src_ref=src.at[pl.ds(rows - HALO, HALO)],
                            dst_ref=halo.at[:, pl.ds(col, src.shape[1])],
                            send_sem=hsend.at[i], recv_sem=hrecv.at[i], device_id={"seq": after}))
    for copy in halos + copies:
        copy.start()

    for src, col in columns:
        pad[8:8 + rows, col:col + src.shape[1]] = src[...].astype(F32)

    def conv(b, col, taps, tcol):
        summed = None
        for j in range(KCONV):
            term = taps[j:j + 1, tcol:tcol + DK].astype(F32) * pad[5 + j + b * C:5 + j + (b + 1) * C, col:col + DK]
            summed = term if summed is None else summed + term
        return silu(summed)

    def unit(u, factor):
        return u * (lax.rsqrt(jnp.sum(u * u, axis=-1, keepdims=True) + 1e-06) * factor)

    def features(b):
        at = slice(b * C, (b + 1) * C)
        for n in range(key_heads):
            cols = slice(n * DK, (n + 1) * DK)
            queries = unit(conv(b, n * DK, cq, n * DK), 1.0 / math.sqrt(DK))
            keys = unit(conv(b, wq + n * DK, ck, n * DK), 1.0)
            uq[at, cols], uk[at, cols] = queries, keys
            keys_s = split(keys)
            kk[n, b] = mm(keys_s, keys_s, NT)
            qk[n, b] = mm(split(queries), keys_s, NT)
        for h in range(heads):
            uv[at, h * DV:(h + 1) * DV] = conv(b, wq + wk + h * DV, cv, h * DV)

    for b in range(1, blocks):
        features(b)
    for copy in halos:
        copy.wait_recv()
    pad[0:8, :] = jnp.where(seq == 0, 0.0, halo[HALO - 8:HALO, :].astype(F32))
    features(0)

    g = part[head]
    for o, copy in enumerate(copies):
        copy.wait_recv()
        g = g + parts[o]

    r, c = iota((C, C), 0), iota((C, C), 1)
    causal, strict = r >= c, r > c
    decays, rates = [], []
    for h in range(heads):
        u = g[2 * h:2 * h + 1, :] + bias[h]
        e = jnp.exp(-jnp.abs(u))
        w = 1.0 + e
        log1p = jnp.where(w == 1.0, e, jnp.log(w) * (e / jnp.where(w == 1.0, 1.0, w - 1.0)))
        decays.append(-scale[h] * (jnp.maximum(u, 0.0) + log1p))
        rates.append(1.0 / (1.0 + jnp.exp(-g[2 * h + 1:2 * h + 2, :])))
    table = jnp.concatenate(decays + rates, axis=0)
    width = table.shape[0]
    table = jnp.concatenate([table[:, b * C:(b + 1) * C] for b in range(blocks)], axis=0)
    cum = lax.dot_general(table, jnp.where(r <= c, 1.0, 0.0), NN, precision=lax.Precision.HIGHEST,
                          preferred_element_type=F32)
    cum_col, rate_col = jnp.transpose(cum), jnp.transpose(table)

    def decay_row(h, b):
        return cum[b * width + h:b * width + h + 1, :]

    def decay_col(h, b):
        return cum_col[:, b * width + h:b * width + h + 1]

    def maps(n):
        every = [(h, b) for b in range(blocks) for h in range(n * group, (n + 1) * group)]
        cols = slice(n * DK, (n + 1) * DK)
        keys = [uk[b * C:(b + 1) * C, cols] for b in range(blocks)]
        systems, betas = [], []
        for h, b in every:
            gap = decay_col(h, b) - decay_row(h, b)
            decay = jnp.where(causal, jnp.exp(jnp.where(causal, gap, 0.0)), 0.0)
            i = b * width + heads + h
            beta = rate_col[:, i:i + 1]
            attend[h, b] = decay * qk[n, b]
            systems.append(jnp.where(strict, beta * decay * kk[n, b], 0.0))
            betas.append(beta)
        solved = inverses(systems, r, c)
        right = []
        for (h, b), beta in zip(every, betas):
            values = uv[b * C:(b + 1) * C, h * DV:(h + 1) * DV]
            right.append(split(jnp.concatenate(
                [(beta * jnp.exp(decay_col(h, b))) * keys[b], beta * values], axis=1)))
        solutions = [mm(split(t), y) for t, y in zip(solved, right)]
        keys_t = [jnp.transpose(y) for y in keys]
        eye = jnp.where(r == c, 1.0, 0.0)
        steps = {}
        for (h, b), y in zip(every, solutions):
            wu[h, b] = y
            last = cum[b * width + h:b * width + h + 1, C - 1:C]
            pair = mm(split(keys_t[b] * jnp.exp(last - decay_row(h, b))), split(y))
            steps[h, b] = (jnp.exp(last) * eye - pair[:, :DK], pair[:, DK:])
        for h in range(n * group, (n + 1) * group):
            now = jnp.concatenate(steps[h, 0], axis=1)
            for b in range(1, blocks):
                xs[h, b - 1] = now
                move, state = then(*steps[h, b], now)
                now = jnp.concatenate([move, state], axis=1)
            ms[h, 0], ms[h, 1] = now[:, :DK], now[:, DK:]

    def to_owner(h):
        return shared(src_ref=ms.at[h], dst_ref=gathered.at[place], send_sem=send1.at[h],
                      recv_sem=recv1.at[place], device_id={"seq": base + seats[h]})

    def hand_over(n):
        for h in range(n * group, (n + 1) * group):
            @pl.when(place != seats[h])
            def _(h=h):
                to_owner(h).start()

            @pl.when(place == seats[h])
            def _(h=h):
                gathered[place] = ms[h]

    def responses(n):
        for h in range(n * group, (n + 1) * group):
            cols = slice(h * DK, (h + 1) * DK)
            for b in range(blocks):
                at = slice(b * C, (b + 1) * C)
                y = wu[h, b]
                queries = jnp.exp(decay_col(h, b)) * uq[at, n * DK:(n + 1) * DK]
                if b == 0:
                    got = mm(split(attend[h, b]), split(y))
                    response, rest = queries - got[:, :DK], got[:, DK:]
                else:
                    now = xs[h, b - 1]
                    z = mm(split(y[:, :DK]), split(now))
                    y = jnp.concatenate([-z[:, :DK], y[:, DK:] - z[:, DK:]], axis=1)
                    got = mm(split(jnp.concatenate([queries, attend[h, b]], axis=1)),
                             split(jnp.concatenate([now, y], axis=0)))
                    response, rest = got[:, :DK], got[:, DK:]
                rhi[at, cols], rlo[at, cols] = split(response)
                out[at, cols] = rest

    maps(0)
    hand_over(0)
    maps(1)
    hand_over(1)
    responses(0)

    def arrive(t):
        @pl.when(place != t)
        def _():
            shared(src_ref=ms.at[0], dst_ref=gathered.at[t], send_sem=send1.at[0], recv_sem=recv1.at[t],
                   device_id={"seq": mirror}).wait_recv()

    arrive(0)
    prefix[0, 0], prefix[0, 1] = gathered[0, 0], gathered[0, 1]
    for t in range(1, GROUP):
        arrive(t)
        move, state = then(gathered[t, 0], gathered[t, 1], wide(prefix, t - 1))
        if t < GROUP - 1:
            prefix[t, 0], prefix[t, 1] = move, state
        else:
            mine[0], mine[1] = move, state

    second = shared(src_ref=mine, dst_ref=other, send_sem=send2, recv_sem=recv2, device_id={"seq": mirror})
    second.start()
    responses(1)
    second.wait_recv()
    a_move, a_state = jnp.where(first_half, mine[0], other[0]), jnp.where(first_half, mine[1], other[1])
    b_move, b_state = jnp.where(first_half, other[0], mine[0]), jnp.where(first_half, other[1], mine[1])
    total[0], total[1] = then(b_move, b_state, jnp.concatenate([a_move, a_state], axis=1))

    def to_row(src, dst, to, i, arrived_at):
        return shared(src_ref=src, dst_ref=dst, send_sem=send3.at[i], recv_sem=recv3.at[arrived_at],
                      device_id={"seq": to * ZROW + z})

    @pl.when(x == 0)
    def _():
        to_row(total.at[1], ein, 1, 0, 0).start()

    @pl.when(x == 2)
    def _():
        to_row(total, tin, 3, 0, 1).start()

    eye = jnp.where(r == c, 1.0, 0.0)
    begin = jnp.concatenate([jnp.where(first_half, eye, a_move), jnp.where(first_half, 0.0, a_state)], axis=1)
    full[0] = begin
    for t in range(1, GROUP):
        full[t] = jnp.concatenate(then(prefix[t - 1, 0], prefix[t - 1, 1], begin), axis=1)

    @pl.when(x == 0)
    def _():
        entry[...] = jnp.zeros_like(entry)

    @pl.when(x > 0)
    def _():
        to_row(total.at[1], ein, 1, 0, 0).wait_recv()

    @pl.when(x == 1)
    def _():
        enext[...] = mm(split(total[0]), split(ein[...])) + total[1]
        to_row(enext, ein, 3, 0, 0).start()
        to_row(enext, ein, 2, 1, 0).start()

    @pl.when((x == 1) | (x == 2))
    def _():
        entry[...] = ein[...]

    @pl.when(x == 3)
    def _():
        to_row(total, tin, 3, 0, 1).wait_recv()
        entry[...] = mm(split(tin[0]), split(ein[...])) + tin[1]

    e_s = split(entry[...])
    for t in range(GROUP):
        staged[t] = mm(split(full[t, :, :DK]), e_s) + full[t, :, DK:]
    last = []
    for o in range(1, GROUP):
        p = lax.rem(place + o, GROUP)
        last.append(shared(src_ref=staged.at[p], dst_ref=arrived.at[own], send_sem=send4.at[o - 1],
                           recv_sem=recv4.at[own], device_id={"seq": base + p}))
    for copy in last:
        copy.start()
    arrived[own] = staged[place]
    for h in range(heads):
        @pl.when(own != h)
        def _(h=h):
            shared(src_ref=staged.at[0], dst_ref=arrived.at[h], send_sem=send4.at[0], recv_sem=recv4.at[h],
                   device_id={"seq": mirror}).wait_recv()
        cols = slice(h * DK, (h + 1) * DK)
        out[:, cols] = out[:, cols] + mm((rhi[:, cols], rlo[:, cols]), split(arrived[h]))

    for copy in copies + halos + [second] + last:
        copy.wait_send()
    for h in range(heads):
        @pl.when(place != seats[h])
        def _(h=h):
            to_owner(h).wait_send()

    @pl.when(x == 0)
    def _():
        to_row(total.at[1], ein, 1, 0, 0).wait_send()

    @pl.when(x == 1)
    def _():
        to_row(enext, ein, 3, 0, 0).wait_send()
        to_row(enext, ein, 2, 1, 0).wait_send()

    @pl.when(x == 2)
    def _():
        to_row(total, tin, 3, 0, 1).wait_send()


def solution(mesh):
    peers, shards = mesh.shape["head"], mesh.shape["seq"]
    rows_x = shards // ZROW
    assert rows_x == 4 and shards == rows_x * ZROW

    def per_device(hid, proj, q, k, v, cq, ck, cv, scale, bias):
        heads, rows = scale.shape[0], q.shape[0]
        key_heads, blocks = q.shape[1] // DK, rows // C
        assert heads == GROUP and rows == blocks * C
        width = q.shape[1] + k.shape[1] + v.shape[1]
        per = proj.shape[1] // peers
        vm, smem = pl.BlockSpec(memory_space=pltpu.VMEM), pl.BlockSpec(memory_space=pltpu.SMEM)
        dma, pair, square = pltpu.SemaphoreType.DMA, (2, DK, DV), (C, C)

        def f32(*shape):
            return pltpu.VMEM(shape, F32)

        return pl.pallas_call(
            functools.partial(whole_kernel, peers, heads, rows_x),
            out_shape=jax.ShapeDtypeStruct((rows, heads * DV), F32),
            in_specs=[smem] * 2 + [vm] * 8,
            out_specs=vm,
            scratch_shapes=[
                f32(peers, per, rows), f32(peers - 1, per, rows), pltpu.VMEM((HALO, width), BF16),
                f32(rows + 8, width), f32(*q.shape), f32(*k.shape), f32(*v.shape),
                f32(key_heads, blocks, *square), f32(key_heads, blocks, *square),
                f32(heads, blocks, *square), f32(heads, blocks, C, DK + DV),
                f32(heads, blocks - 1, DK, DK + DV), f32(heads, *pair),
                pltpu.VMEM((rows, heads * DK), BF16), pltpu.VMEM((rows, heads * DK), BF16),
                f32(GROUP, *pair), f32(GROUP - 1, *pair), f32(*pair), f32(*pair), f32(*pair), f32(*pair),
                f32(DK, DV), f32(DK, DV), f32(DK, DV), f32(GROUP, DK, DK + DV),
                f32(GROUP, DK, DV), f32(GROUP, DK, DV),
                dma((peers - 1,)), dma((peers - 1,)), dma((3,)), dma((3,)),
                dma((heads,)), dma((GROUP,)), dma, dma, dma((2,)), dma((2,)),
                dma((GROUP - 1,)), dma((GROUP,)),
            ],
            compiler_params=pltpu.CompilerParams(collective_id=0, has_side_effects=True),
            name="delta",
        )(scale, bias, hid, jnp.transpose(proj), q, k, v, cq, ck, cv)

    placed = (
        P("seq", "head"), P("head", None), P("seq", "head"), P("seq", "head"), P("seq", "head"),
        P(None, "head"), P(None, "head"), P(None, "head"), P("head"), P("head"),
    )
    return jax.shard_map(per_device, mesh=mesh, in_specs=placed, out_specs=P("seq", "head"), check_vma=False)
```

```python
import functools
import math

import jax
import jax.numpy as jnp
from jax import lax
from jax.experimental import pallas as pl
from jax.experimental.pallas import tpu as pltpu
from jax.sharding import PartitionSpec as P

DK = 128
DV = 128
KCONV = 4
C = 128
ZROW = 8
GROUP = 4
HALO = 16

MESH = pl.DeviceIdType.MESH
F32 = jnp.float32
BF16 = jnp.bfloat16


def split(a):
    hi = a.astype(BF16)
    return hi, (a - hi.astype(F32)).astype(BF16)


NN = (((1,), (0,)), ((), ()))
NT = (((1,), (1,)), ((), ()))


def mm(a, b, dims=NN):
    dot = functools.partial(lax.dot_general, dimension_numbers=dims, preferred_element_type=F32)
    if dims is NN and a[0].shape[1] == 128:
        pair = jnp.concatenate(a, axis=1)
        hi, lo = (jnp.concatenate([x, x], axis=0) for x in b)
        return dot(pair, hi) + dot(pair, lo)
    return dot(a[0], b[0]) + (dot(a[0], b[1]) + dot(a[1], b[0]))


def iota(shape, axis):
    return lax.broadcasted_iota(jnp.int32, shape, axis)


def silu(u):
    return u / (1.0 + jnp.exp(-u))


def inverses(systems, r, c):
    lane, sub = iota((8, C), 1), iota((8, C), 0)
    group = lane >> 3
    solved = []
    for a in systems:
        packed = a[0:8, :]
        for j in range(1, C // 8):
            packed = jnp.where(group == j, a[8 * j:8 * j + 8, :], packed)
        t = jnp.where((lane & 7) == sub, 1.0, 0.0)
        for m in range(7):
            factor = jnp.take_along_axis(packed, (lane & ~7) + m, axis=1)
            t = t - factor * t[m:m + 1, :]
        solved.append(jnp.concatenate([jnp.where(group == j, t, 0.0) for j in range(C // 8)], axis=0))
    for level in range(3, 7):
        off = ((r >> (level + 1)) == (c >> (level + 1))) & ((r >> level) != (c >> level))
        parts = [split(t) for t in solved]
        inner = [mm(split(jnp.where(off, a, 0.0)), ts) for a, ts in zip(systems, parts)]
        solved = [t - mm(ts, split(p)) for t, ts, p in zip(solved, parts, inner)]
    return solved


def wide(ref, *at):
    return jnp.concatenate([ref[(*at, 0)], ref[(*at, 1)]], axis=1)


def then(later_move, later_state, x):
    y = mm(split(later_move), split(x))
    return y[:, :DK], y[:, DK:] + later_state


SEAT = (0, 3, 1, 2)


def owned_at(p):
    return jnp.where(p == 0, 0, jnp.where(p == GROUP - 1, 1, p + 1))


def whole_kernel(peers, heads, rows_x, scale, bias, cq, ck, cv, hid_in, proj_in, q_in, k_in, v_in, out,
                 hid, proj, q, k, v, load,
                 part, parts, halo, pad, uq, uk, uv, kk, qk, attend, wu, xs, ms, rhi, rlo,
                 gathered, prefix, mine, other, total, tin, ein, begin, enext, full, staged, arrived,
                 send, recv, hsend, hrecv, send1, recv1, send2, recv2, send3, recv3, send4, recv4):
    seq, head = lax.axis_index("seq"), lax.axis_index("head")
    shards = rows_x * ZROW
    z, x = lax.rem(seq, ZROW), seq // ZROW
    half, place = z // GROUP, lax.rem(z, GROUP)
    first_half = half == 0
    base = seq - place
    mirror = x * ZROW + (ZROW - 1 - z)
    after, before = lax.rem(seq + 1, shards), lax.rem(seq + shards - 1, shards)
    own = owned_at(jnp.where(first_half, place, GROUP - 1 - place))
    seats = [jnp.where(first_half, SEAT[h], GROUP - 1 - SEAT[h]) for h in range(heads)]
    rows, wq, wk = q.shape[0], q.shape[1], k.shape[1]
    blocks, key_heads = rows // C, wq // DK
    group = heads // key_heads
    shared = functools.partial(pltpu.make_async_remote_copy, device_id_type=MESH)

    barrier = pltpu.get_barrier_semaphore()
    for o in range(1, peers):
        pl.semaphore_signal(barrier, inc=1, device_id={"head": lax.rem(head + o, peers)}, device_id_type=MESH)
    others = [after, before, mirror]
    others += [base + lax.rem(place + o, GROUP) for o in range(1, GROUP)]
    others += [lax.rem(x + o, rows_x) * ZROW + z for o in range(1, rows_x)]
    for s in others:
        pl.semaphore_signal(barrier, inc=1, device_id={"seq": s}, device_id_type=MESH)

    loads = [pltpu.make_async_copy(src, dst, load.at[i]) for i, (src, dst) in enumerate(
        [(hid_in, hid), (proj_in, proj), (q_in, q), (k_in, k), (v_in, v)])]
    for copy in loads:
        copy.start()
    for copy in loads[:2]:
        copy.wait()
    flat = lax.dot_general(proj[...], hid[...], NT, preferred_element_type=F32)
    per = flat.shape[0] // peers
    for p in range(peers):
        part[p] = flat[p * per:(p + 1) * per, :]
    for copy in loads[2:]:
        copy.wait()
    pl.semaphore_wait(barrier, peers - 1 + len(others))
    copies = []
    for o in range(1, peers):
        to = lax.rem(head + o, peers)
        copies.append(shared(src_ref=part.at[to], dst_ref=parts.at[o - 1], send_sem=send.at[o - 1],
                             recv_sem=recv.at[o - 1], device_id={"head": to}))
    columns = [(q, 0), (k, wq), (v, wq + wk)]
    halos = []
    for i, (src, col) in enumerate(columns):
        halos.append(shared(src_ref=src.at[pl.ds(rows - HALO, HALO)],
                            dst_ref=halo.at[:, pl.ds(col, src.shape[1])],
                            send_sem=hsend.at[i], recv_sem=hrecv.at[i], device_id={"seq": after}))
    for copy in halos + copies:
        copy.start()

    for src, col in columns:
        pad[8:8 + rows, col:col + src.shape[1]] = src[...].astype(F32)

    def conv(b, col, taps, tcol):
        summed = None
        for j in range(KCONV):
            term = taps[j:j + 1, tcol:tcol + DK].astype(F32) * pad[5 + j + b * C:5 + j + (b + 1) * C, col:col + DK]
            summed = term if summed is None else summed + term
        return silu(summed)

    def unit(u, factor):
        return u * (lax.rsqrt(jnp.sum(u * u, axis=-1, keepdims=True) + 1e-06) * factor)

    def features(b):
        at = slice(b * C, (b + 1) * C)
        for n in range(key_heads):
            cols = slice(n * DK, (n + 1) * DK)
            queries = unit(conv(b, n * DK, cq, n * DK), 1.0 / math.sqrt(DK))
            keys = unit(conv(b, wq + n * DK, ck, n * DK), 1.0)
            uq[at, cols], uk[at, cols] = queries, keys
            keys_s = split(keys)
            kk[n, b] = mm(keys_s, keys_s, NT)
            qk[n, b] = mm(split(queries), keys_s, NT)
        for h in range(heads):
            uv[at, h * DV:(h + 1) * DV] = conv(b, wq + wk + h * DV, cv, h * DV)

    for b in range(1, blocks):
        features(b)
    for copy in halos:
        copy.wait_recv()
    pad[0:8, :] = jnp.where(seq == 0, 0.0, halo[HALO - 8:HALO, :].astype(F32))
    features(0)

    g = part[head]
    for o, copy in enumerate(copies):
        copy.wait_recv()
        g = g + parts[o]

    r, c = iota((C, C), 0), iota((C, C), 1)
    causal, strict = r >= c, r > c
    decays, rates = [], []
    for h in range(heads):
        u = g[2 * h:2 * h + 1, :] + bias[h]
        e = jnp.exp(-jnp.abs(u))
        w = 1.0 + e
        log1p = jnp.where(w == 1.0, e, jnp.log(w) * (e / jnp.where(w == 1.0, 1.0, w - 1.0)))
        decays.append(-scale[h] * (jnp.maximum(u, 0.0) + log1p))
        rates.append(1.0 / (1.0 + jnp.exp(-g[2 * h + 1:2 * h + 2, :])))
    table = jnp.concatenate(decays + rates, axis=0)
    width = table.shape[0]
    table = jnp.concatenate([table[:, b * C:(b + 1) * C] for b in range(blocks)], axis=0)
    cum = lax.dot_general(table, jnp.where(r <= c, 1.0, 0.0), NN, precision=lax.Precision.HIGHEST,
                          preferred_element_type=F32)
    cum_col, rate_col = jnp.transpose(cum), jnp.transpose(table)

    def decay_row(h, b):
        return cum[b * width + h:b * width + h + 1, :]

    def decay_col(h, b):
        return cum_col[:, b * width + h:b * width + h + 1]

    def maps(n):
        every = [(h, b) for b in range(blocks) for h in range(n * group, (n + 1) * group)]
        cols = slice(n * DK, (n + 1) * DK)
        keys = [uk[b * C:(b + 1) * C, cols] for b in range(blocks)]
        systems, betas = [], []
        for h, b in every:
            gap = decay_col(h, b) - decay_row(h, b)
            decay = jnp.where(causal, jnp.exp(jnp.where(causal, gap, 0.0)), 0.0)
            i = b * width + heads + h
            beta = rate_col[:, i:i + 1]
            attend[h, b] = decay * qk[n, b]
            systems.append(jnp.where(strict, beta * decay * kk[n, b], 0.0))
            betas.append(beta)
        solved = inverses(systems, r, c)
        right = []
        for (h, b), beta in zip(every, betas):
            values = uv[b * C:(b + 1) * C, h * DV:(h + 1) * DV]
            right.append(split(jnp.concatenate(
                [(beta * jnp.exp(decay_col(h, b))) * keys[b], beta * values], axis=1)))
        solutions = [mm(split(t), y) for t, y in zip(solved, right)]
        keys_t = [jnp.transpose(y) for y in keys]
        eye = jnp.where(r == c, 1.0, 0.0)
        steps = {}
        for (h, b), y in zip(every, solutions):
            wu[h, b] = y
            last = cum[b * width + h:b * width + h + 1, C - 1:C]
            pair = mm(split(keys_t[b] * jnp.exp(last - decay_row(h, b))), split(y))
            steps[h, b] = (jnp.exp(last) * eye - pair[:, :DK], pair[:, DK:])
        for h in range(n * group, (n + 1) * group):
            now = jnp.concatenate(steps[h, 0], axis=1)
            for b in range(1, blocks):
                xs[h, b - 1] = now
                move, state = then(*steps[h, b], now)
                now = jnp.concatenate([move, state], axis=1)
            ms[h, 0], ms[h, 1] = now[:, :DK], now[:, DK:]

    def to_owner(h):
        return shared(src_ref=ms.at[h], dst_ref=gathered.at[place], send_sem=send1.at[h],
                      recv_sem=recv1.at[place], device_id={"seq": base + seats[h]})

    def hand_over(n):
        for h in range(n * group, (n + 1) * group):
            @pl.when(place != seats[h])
            def _(h=h):
                to_owner(h).start()

            @pl.when(place == seats[h])
            def _(h=h):
                gathered[place] = ms[h]

    def responses(n):
        for h in range(n * group, (n + 1) * group):
            cols = slice(h * DK, (h + 1) * DK)
            for b in range(blocks):
                at = slice(b * C, (b + 1) * C)
                y = wu[h, b]
                queries = jnp.exp(decay_col(h, b)) * uq[at, n * DK:(n + 1) * DK]
                if b == 0:
                    got = mm(split(attend[h, b]), split(y))
                    response, rest = queries - got[:, :DK], got[:, DK:]
                else:
                    now = xs[h, b - 1]
                    z = mm(split(y[:, :DK]), split(now))
                    y = jnp.concatenate([-z[:, :DK], y[:, DK:] - z[:, DK:]], axis=1)
                    got = mm(split(jnp.concatenate([queries, attend[h, b]], axis=1)),
                             split(jnp.concatenate([now, y], axis=0)))
                    response, rest = got[:, :DK], got[:, DK:]
                rhi[at, cols], rlo[at, cols] = split(response)
                out[at, cols] = rest

    maps(0)
    hand_over(0)
    maps(1)
    hand_over(1)
    responses(0)

    def arrive(t):
        @pl.when(place != t)
        def _():
            shared(src_ref=ms.at[0], dst_ref=gathered.at[t], send_sem=send1.at[0], recv_sem=recv1.at[t],
                   device_id={"seq": mirror}).wait_recv()

    arrive(0)
    arrive(1)
    early = jnp.concatenate(then(gathered[1, 0], gathered[1, 1], wide(gathered, 0)), axis=1)
    arrive(2)
    arrive(3)
    late = then(gathered[3, 0], gathered[3, 1], wide(gathered, 2))
    mine[0], mine[1] = then(*late, early)

    def to_mirror(i):
        return shared(src_ref=mine.at[i], dst_ref=other.at[i], send_sem=send2.at[i], recv_sem=recv2.at[i],
                      device_id={"seq": mirror})

    lead = jnp.where(first_half, 1, 0)
    to_mirror(lead).start()
    to_mirror(1 - lead).start()
    prefix[0, 0], prefix[0, 1] = gathered[0, 0], gathered[0, 1]
    prefix[1, 0], prefix[1, 1] = early[:, :DK], early[:, DK:]
    prefix[2, 0], prefix[2, 1] = then(gathered[2, 0], gathered[2, 1], early)
    responses(1)

    @pl.when(first_half)
    def _():
        to_mirror(0).wait_recv()
        y = mm(split(other[0]), split(wide(mine)))
        total[0] = y[:, :DK]
        to_mirror(1).wait_recv()
        total[1] = y[:, DK:] + other[1]

    @pl.when(half == 1)
    def _():
        to_mirror(1).wait_recv()
        total[1] = mm(split(mine[0]), split(other[1])) + mine[1]

    def to_row(src, dst, to, i, arrived_at):
        return shared(src_ref=src, dst_ref=dst, send_sem=send3.at[i], recv_sem=recv3.at[arrived_at],
                      device_id={"seq": to * ZROW + z})

    @pl.when(x == 0)
    def _():
        to_row(total.at[1], ein, 1, 0, 0).start()

    @pl.when(half == 1)
    def _():
        to_mirror(0).wait_recv()
        total[0] = mm(split(mine[0]), split(other[0]))

    @pl.when(x == 2)
    def _():
        to_row(total, tin, 3, 0, 1).start()

    eye = jnp.where(r == c, 1.0, 0.0)
    begin[0] = jnp.where(first_half, eye, other[0])
    begin[1] = jnp.where(first_half, 0.0, other[1])

    @pl.when(x == 3)
    def _():
        to_row(total, tin, 3, 0, 1).wait_recv()
        begin[0], begin[1] = then(begin[0], begin[1], wide(tin))

    start_s = split(wide(begin))
    full[0] = wide(begin)
    for t in range(1, GROUP):
        y = mm(split(prefix[t - 1, 0]), start_s)
        full[t] = jnp.concatenate([y[:, :DK], y[:, DK:] + prefix[t - 1, 1]], axis=1)

    @pl.when(x == 0)
    def _():
        ein[...] = jnp.zeros_like(ein)

    @pl.when(x > 0)
    def _():
        to_row(total.at[1], ein, 1, 0, 0).wait_recv()

    @pl.when(x == 1)
    def _():
        enext[...] = mm(split(total[0]), split(ein[...])) + total[1]
        to_row(enext, ein, 3, 0, 0).start()
        to_row(enext, ein, 2, 1, 0).start()

    e_s = split(ein[...])

    def stage(t):
        staged[t] = mm(split(full[t, :, :DK]), e_s) + full[t, :, DK:]

    last = []
    for o in range(1, GROUP):
        p = lax.rem(place + o, GROUP)
        stage(p)
        last.append(shared(src_ref=staged.at[p], dst_ref=arrived.at[own], send_sem=send4.at[o - 1],
                           recv_sem=recv4.at[own], device_id={"seq": base + p}))
        last[-1].start()
    stage(place)
    arrived[own] = staged[place]
    for h in range(heads):
        @pl.when(own != h)
        def _(h=h):
            shared(src_ref=staged.at[0], dst_ref=arrived.at[h], send_sem=send4.at[0], recv_sem=recv4.at[h],
                   device_id={"seq": mirror}).wait_recv()
        cols = slice(h * DK, (h + 1) * DK)
        out[:, cols] = out[:, cols] + mm((rhi[:, cols], rlo[:, cols]), split(arrived[h]))

    for copy in copies + halos + [to_mirror(0), to_mirror(1)] + last:
        copy.wait_send()
    for h in range(heads):
        @pl.when(place != seats[h])
        def _(h=h):
            to_owner(h).wait_send()

    @pl.when(x == 0)
    def _():
        to_row(total.at[1], ein, 1, 0, 0).wait_send()

    @pl.when(x == 1)
    def _():
        to_row(enext, ein, 3, 0, 0).wait_send()
        to_row(enext, ein, 2, 1, 0).wait_send()

    @pl.when(x == 2)
    def _():
        to_row(total, tin, 3, 0, 1).wait_send()


def solution(mesh):
    peers, shards = mesh.shape["head"], mesh.shape["seq"]
    rows_x = shards // ZROW
    assert rows_x == 4 and shards == rows_x * ZROW

    def per_device(hid, proj, q, k, v, cq, ck, cv, scale, bias):
        heads, rows = scale.shape[0], q.shape[0]
        key_heads, blocks = q.shape[1] // DK, rows // C
        assert heads == GROUP and rows == blocks * C
        width = q.shape[1] + k.shape[1] + v.shape[1]
        per = proj.shape[1] // peers
        proj = jnp.transpose(proj)
        vm, smem = pl.BlockSpec(memory_space=pltpu.VMEM), pl.BlockSpec(memory_space=pltpu.SMEM)
        dma, pair, square = pltpu.SemaphoreType.DMA, (2, DK, DV), (C, C)

        def f32(*shape):
            return pltpu.VMEM(shape, F32)

        return pl.pallas_call(
            functools.partial(whole_kernel, peers, heads, rows_x),
            out_shape=jax.ShapeDtypeStruct((rows, heads * DV), F32),
            in_specs=[smem] * 2 + [vm] * 3 + [pl.BlockSpec(memory_space=pltpu.HBM)] * 5,
            out_specs=vm,
            scratch_shapes=[
                *(pltpu.VMEM(a.shape, BF16) for a in (hid, proj, q, k, v)), dma((5,)),
                f32(peers, per, rows), f32(peers - 1, per, rows), pltpu.VMEM((HALO, width), BF16),
                f32(rows + 8, width), f32(*q.shape), f32(*k.shape), f32(*v.shape),
                f32(key_heads, blocks, *square), f32(key_heads, blocks, *square),
                f32(heads, blocks, *square), f32(heads, blocks, C, DK + DV),
                f32(heads, blocks - 1, DK, DK + DV), f32(heads, *pair),
                pltpu.VMEM((rows, heads * DK), BF16), pltpu.VMEM((rows, heads * DK), BF16),
                f32(GROUP, *pair), f32(GROUP - 1, *pair), f32(*pair), f32(*pair), f32(*pair), f32(*pair),
                f32(DK, DV), f32(*pair), f32(DK, DV), f32(GROUP, DK, DK + DV),
                f32(GROUP, DK, DV), f32(GROUP, DK, DV),
                dma((peers - 1,)), dma((peers - 1,)), dma((3,)), dma((3,)),
                dma((heads,)), dma((GROUP,)), dma((2,)), dma((2,)), dma((2,)), dma((2,)),
                dma((GROUP - 1,)), dma((GROUP,)),
            ],
            compiler_params=pltpu.CompilerParams(collective_id=0, has_side_effects=True),
            name="delta",
        )(scale, bias, cq, ck, cv, hid, proj, q, k, v)

    placed = (
        P("seq", "head"), P("head", None), P("seq", "head"), P("seq", "head"), P("seq", "head"),
        P(None, "head"), P(None, "head"), P(None, "head"), P("head"), P("head"),
    )
    return jax.shard_map(per_device, mesh=mesh, in_specs=placed, out_specs=P("seq", "head"), check_vma=False)
```

```python
import functools
import math

import jax
import jax.numpy as jnp
from jax import lax
from jax.experimental import pallas as pl
from jax.experimental.pallas import tpu as pltpu
from jax.sharding import PartitionSpec as P

DK = 128
DV = 128
KCONV = 4
C = 128
ZROW = 8
GROUP = 4
BASE = 8
HALO = 16

MESH = pl.DeviceIdType.MESH
F32 = jnp.float32
BF16 = jnp.bfloat16


def split(a):
    hi = a.astype(BF16)
    return hi, (a - hi.astype(F32)).astype(BF16)


NN = (((1,), (0,)), ((), ()))
NT = (((1,), (1,)), ((), ()))


def mm(a, b, dims=NN):
    dot = functools.partial(lax.dot_general, dimension_numbers=dims, preferred_element_type=F32)
    if dims is NN and a[0].shape[1] == 128:
        pair = jnp.concatenate(a, axis=1)
        hi, lo = (jnp.concatenate([x, x], axis=0) for x in b)
        return dot(pair, hi) + dot(pair, lo)
    return dot(a[0], b[0]) + (dot(a[0], b[1]) + dot(a[1], b[0]))


def iota(shape, axis):
    return lax.broadcasted_iota(jnp.int32, shape, axis)


def silu(u):
    return u / (1.0 + jnp.exp(-u))


def inverses(systems):
    lane, sub = iota((BASE, C), 1), iota((BASE, C), 0)
    group, within = lane // BASE, lane & (BASE - 1)
    solved = []
    for a in systems:
        packed = a[0:BASE, :]
        for j in range(1, C // BASE):
            packed = jnp.where(group == j, a[BASE * j:BASE * (j + 1), :], packed)
        tops = [jnp.where(within[i:i + 8] == sub[i:i + 8], 1.0, 0.0) for i in range(0, BASE, 8)]
        for m in range(BASE - 1):
            row = tops[m // 8][m % 8:m % 8 + 1, :]
            for i in range((m + 1) // 8, BASE // 8):
                factor = jnp.take_along_axis(packed[8 * i:8 * i + 8], (lane[:8] - within[:8]) + m, axis=1)
                tops[i] = tops[i] - factor * row
        t = jnp.concatenate(tops, axis=0)
        solved.append(jnp.concatenate([jnp.where(group == j, t, 0.0) for j in range(C // BASE)], axis=0))
    size = BASE
    while size < C:
        count = C // (2 * size)

        def lower(x):
            return jnp.concatenate([x[(2 * j + 1) * size:(2 * j + 2) * size] for j in range(count)], axis=0)

        def weave(upper, low):
            pieces = []
            for j in range(count):
                pieces.append(upper[2 * j * size:(2 * j + 1) * size])
                pieces.append(low[j * size:(j + 1) * size])
            return jnp.concatenate(pieces, axis=0)

        rows, cols = iota((C // 2, C), 0) // size, iota((C // 2, C), 1) // size
        left = cols == 2 * rows
        parts = [split(t) for t in solved]
        inner = [mm(split(jnp.where(left, lower(a), 0.0)), ts) for a, ts in zip(systems, parts)]
        zeros = jnp.zeros((C, C), F32)
        step = [mm(split(lower(t)), split(weave(zeros, p))) for t, p in zip(solved, inner)]
        solved = [weave(t, lower(t) - y) for t, y in zip(solved, step)]
        size *= 2
    return solved


def wide(ref, *at):
    return jnp.concatenate([ref[(*at, 0)], ref[(*at, 1)]], axis=1)


def then(later_move, later_state, x):
    y = mm(split(later_move), split(x))
    return y[:, :DK], y[:, DK:] + later_state


SEAT = (0, 3, 1, 2)


def owned_at(p):
    return jnp.where(p == 0, 0, jnp.where(p == GROUP - 1, 1, p + 1))


def whole_kernel(peers, heads, rows_x, scale, bias, cq, ck, cv, hid_in, proj_in, q_in, k_in, v_in, out,
                 hid, proj, q, k, v, load,
                 part, parts, halo, pad, uq, uk, uv, kk, qk, attend, wu, xs, ms, rhi, rlo,
                 gathered, prefix, mine, other, total, tin, ein, begin, enext, full, staged, arrived,
                 send, recv, hsend, hrecv, send1, recv1, send2, recv2, send3, recv3, send4, recv4):
    seq, head = lax.axis_index("seq"), lax.axis_index("head")
    shards = rows_x * ZROW
    z, x = lax.rem(seq, ZROW), seq // ZROW
    half, place = z // GROUP, lax.rem(z, GROUP)
    first_half = half == 0
    base = seq - place
    mirror = x * ZROW + (ZROW - 1 - z)
    after, before = lax.rem(seq + 1, shards), lax.rem(seq + shards - 1, shards)
    own = owned_at(jnp.where(first_half, place, GROUP - 1 - place))
    seats = [jnp.where(first_half, SEAT[h], GROUP - 1 - SEAT[h]) for h in range(heads)]
    rows, wq, wk = q.shape[0], q.shape[1], k.shape[1]
    blocks, key_heads = rows // C, wq // DK
    group = heads // key_heads
    shared = functools.partial(pltpu.make_async_remote_copy, device_id_type=MESH)

    barrier = pltpu.get_barrier_semaphore()
    for o in range(1, peers):
        pl.semaphore_signal(barrier, inc=1, device_id={"head": lax.rem(head + o, peers)}, device_id_type=MESH)
    others = [after, before, mirror]
    others += [base + lax.rem(place + o, GROUP) for o in range(1, GROUP)]
    others += [lax.rem(x + o, rows_x) * ZROW + z for o in range(1, rows_x)]
    for s in others:
        pl.semaphore_signal(barrier, inc=1, device_id={"seq": s}, device_id_type=MESH)

    loads = [pltpu.make_async_copy(src, dst, load.at[i]) for i, (src, dst) in enumerate(
        [(hid_in, hid), (proj_in, proj), (q_in, q), (k_in, k), (v_in, v)])]
    for copy in loads:
        copy.start()
    for copy in loads[:2]:
        copy.wait()
    flat = lax.dot_general(proj[...], hid[...], NT, preferred_element_type=F32)
    per = flat.shape[0] // peers
    for p in range(peers):
        part[p] = flat[p * per:(p + 1) * per, :]
    for copy in loads[2:]:
        copy.wait()
    pl.semaphore_wait(barrier, peers - 1 + len(others))
    copies = []
    for o in range(1, peers):
        to = lax.rem(head + o, peers)
        copies.append(shared(src_ref=part.at[to], dst_ref=parts.at[o - 1], send_sem=send.at[o - 1],
                             recv_sem=recv.at[o - 1], device_id={"head": to}))
    columns = [(q, 0), (k, wq), (v, wq + wk)]
    halos = []
    for i, (src, col) in enumerate(columns):
        halos.append(shared(src_ref=src.at[pl.ds(rows - HALO, HALO)],
                            dst_ref=halo.at[:, pl.ds(col, src.shape[1])],
                            send_sem=hsend.at[i], recv_sem=hrecv.at[i], device_id={"seq": after}))
    for copy in halos + copies:
        copy.start()

    for src, col in columns:
        pad[8:8 + rows, col:col + src.shape[1]] = src[...].astype(F32)

    def conv(b, col, taps, tcol):
        summed = None
        for j in range(KCONV):
            term = taps[j:j + 1, tcol:tcol + DK].astype(F32) * pad[5 + j + b * C:5 + j + (b + 1) * C, col:col + DK]
            summed = term if summed is None else summed + term
        return silu(summed)

    def unit(u, factor):
        return u * (lax.rsqrt(jnp.sum(u * u, axis=-1, keepdims=True) + 1e-06) * factor)

    def features(b):
        at = slice(b * C, (b + 1) * C)
        for n in range(key_heads):
            cols = slice(n * DK, (n + 1) * DK)
            queries = unit(conv(b, n * DK, cq, n * DK), 1.0 / math.sqrt(DK))
            keys = unit(conv(b, wq + n * DK, ck, n * DK), 1.0)
            uq[at, cols], uk[at, cols] = queries, keys
            keys_s = split(keys)
            kk[n, b] = mm(keys_s, keys_s, NT)
            qk[n, b] = mm(split(queries), keys_s, NT)
        for h in range(heads):
            uv[at, h * DV:(h + 1) * DV] = conv(b, wq + wk + h * DV, cv, h * DV)

    for b in range(1, blocks):
        features(b)
    for copy in halos:
        copy.wait_recv()
    pad[0:8, :] = jnp.where(seq == 0, 0.0, halo[HALO - 8:HALO, :].astype(F32))
    features(0)

    g = part[head]
    for o, copy in enumerate(copies):
        copy.wait_recv()
        g = g + parts[o]

    r, c = iota((C, C), 0), iota((C, C), 1)
    causal, strict = r >= c, r > c
    decays, rates = [], []
    for h in range(heads):
        u = g[2 * h:2 * h + 1, :] + bias[h]
        e = jnp.exp(-jnp.abs(u))
        w = 1.0 + e
        log1p = jnp.where(w == 1.0, e, jnp.log(w) * (e / jnp.where(w == 1.0, 1.0, w - 1.0)))
        decays.append(-scale[h] * (jnp.maximum(u, 0.0) + log1p))
        rates.append(1.0 / (1.0 + jnp.exp(-g[2 * h + 1:2 * h + 2, :])))
    table = jnp.concatenate(decays + rates, axis=0)
    width = table.shape[0]
    table = jnp.concatenate([table[:, b * C:(b + 1) * C] for b in range(blocks)], axis=0)
    cum = lax.dot_general(table, jnp.where(r <= c, 1.0, 0.0), NN, precision=lax.Precision.HIGHEST,
                          preferred_element_type=F32)
    cum_col, rate_col = jnp.transpose(cum), jnp.transpose(table)

    def decay_row(h, b):
        return cum[b * width + h:b * width + h + 1, :]

    def decay_col(h, b):
        return cum_col[:, b * width + h:b * width + h + 1]

    def maps(n):
        every = [(h, b) for b in range(blocks) for h in range(n * group, (n + 1) * group)]
        cols = slice(n * DK, (n + 1) * DK)
        keys = [uk[b * C:(b + 1) * C, cols] for b in range(blocks)]
        systems, betas = [], []
        for h, b in every:
            gap = decay_col(h, b) - decay_row(h, b)
            decay = jnp.where(causal, jnp.exp(jnp.where(causal, gap, 0.0)), 0.0)
            i = b * width + heads + h
            beta = rate_col[:, i:i + 1]
            attend[h, b] = decay * qk[n, b]
            systems.append(jnp.where(strict, beta * decay * kk[n, b], 0.0))
            betas.append(beta)
        solved = inverses(systems)
        right = []
        for (h, b), beta in zip(every, betas):
            values = uv[b * C:(b + 1) * C, h * DV:(h + 1) * DV]
            right.append(split(jnp.concatenate(
                [(beta * jnp.exp(decay_col(h, b))) * keys[b], beta * values], axis=1)))
        solutions = [mm(split(t), y) for t, y in zip(solved, right)]
        keys_t = [jnp.transpose(y) for y in keys]
        eye = jnp.where(r == c, 1.0, 0.0)
        steps = {}
        for (h, b), y in zip(every, solutions):
            wu[h, b] = y
            last = cum[b * width + h:b * width + h + 1, C - 1:C]
            pair = mm(split(keys_t[b] * jnp.exp(last - decay_row(h, b))), split(y))
            steps[h, b] = (jnp.exp(last) * eye - pair[:, :DK], pair[:, DK:])
        for h in range(n * group, (n + 1) * group):
            now = jnp.concatenate(steps[h, 0], axis=1)
            for b in range(1, blocks):
                xs[h, b - 1] = now
                move, state = then(*steps[h, b], now)
                now = jnp.concatenate([move, state], axis=1)
            ms[h, 0], ms[h, 1] = now[:, :DK], now[:, DK:]

    def to_owner(h):
        return shared(src_ref=ms.at[h], dst_ref=gathered.at[place], send_sem=send1.at[h],
                      recv_sem=recv1.at[place], device_id={"seq": base + seats[h]})

    def hand_over(n):
        for h in range(n * group, (n + 1) * group):
            @pl.when(place != seats[h])
            def _(h=h):
                to_owner(h).start()

            @pl.when(place == seats[h])
            def _(h=h):
                gathered[place] = ms[h]

    def responses(n):
        for h in range(n * group, (n + 1) * group):
            cols = slice(h * DK, (h + 1) * DK)
            for b in range(blocks):
                at = slice(b * C, (b + 1) * C)
                y = wu[h, b]
                queries = jnp.exp(decay_col(h, b)) * uq[at, n * DK:(n + 1) * DK]
                if b == 0:
                    got = mm(split(attend[h, b]), split(y))
                    response, rest = queries - got[:, :DK], got[:, DK:]
                else:
                    now = xs[h, b - 1]
                    z = mm(split(y[:, :DK]), split(now))
                    y = jnp.concatenate([-z[:, :DK], y[:, DK:] - z[:, DK:]], axis=1)
                    got = mm(split(jnp.concatenate([queries, attend[h, b]], axis=1)),
                             split(jnp.concatenate([now, y], axis=0)))
                    response, rest = got[:, :DK], got[:, DK:]
                rhi[at, cols], rlo[at, cols] = split(response)
                out[at, cols] = rest

    maps(0)
    hand_over(0)
    maps(1)
    hand_over(1)
    responses(0)

    def arrive(t):
        @pl.when(place != t)
        def _():
            shared(src_ref=ms.at[0], dst_ref=gathered.at[t], send_sem=send1.at[0], recv_sem=recv1.at[t],
                   device_id={"seq": mirror}).wait_recv()

    arrive(0)
    arrive(1)
    early = jnp.concatenate(then(gathered[1, 0], gathered[1, 1], wide(gathered, 0)), axis=1)
    arrive(2)
    arrive(3)
    late = then(gathered[3, 0], gathered[3, 1], wide(gathered, 2))
    mine[0], mine[1] = then(*late, early)

    def to_mirror(i):
        return shared(src_ref=mine.at[i], dst_ref=other.at[i], send_sem=send2.at[i], recv_sem=recv2.at[i],
                      device_id={"seq": mirror})

    lead = jnp.where(first_half, 1, 0)
    to_mirror(lead).start()
    to_mirror(1 - lead).start()
    prefix[0, 0], prefix[0, 1] = gathered[0, 0], gathered[0, 1]
    prefix[1, 0], prefix[1, 1] = early[:, :DK], early[:, DK:]
    prefix[2, 0], prefix[2, 1] = then(gathered[2, 0], gathered[2, 1], early)
    responses(1)

    @pl.when(first_half)
    def _():
        to_mirror(0).wait_recv()
        y = mm(split(other[0]), split(wide(mine)))
        total[0] = y[:, :DK]
        to_mirror(1).wait_recv()
        total[1] = y[:, DK:] + other[1]

    @pl.when(half == 1)
    def _():
        to_mirror(1).wait_recv()
        total[1] = mm(split(mine[0]), split(other[1])) + mine[1]

    def to_row(src, dst, to, i, arrived_at):
        return shared(src_ref=src, dst_ref=dst, send_sem=send3.at[i], recv_sem=recv3.at[arrived_at],
                      device_id={"seq": to * ZROW + z})

    @pl.when(x == 0)
    def _():
        to_row(total.at[1], ein, 1, 0, 0).start()

    @pl.when(half == 1)
    def _():
        to_mirror(0).wait_recv()
        total[0] = mm(split(mine[0]), split(other[0]))

    @pl.when(x == 2)
    def _():
        to_row(total, tin, 3, 0, 1).start()

    eye = jnp.where(r == c, 1.0, 0.0)
    begin[0] = jnp.where(first_half, eye, other[0])
    begin[1] = jnp.where(first_half, 0.0, other[1])

    @pl.when(x == 3)
    def _():
        to_row(total, tin, 3, 0, 1).wait_recv()
        begin[0], begin[1] = then(begin[0], begin[1], wide(tin))

    start_s = split(wide(begin))
    full[0] = wide(begin)
    for t in range(1, GROUP):
        y = mm(split(prefix[t - 1, 0]), start_s)
        full[t] = jnp.concatenate([y[:, :DK], y[:, DK:] + prefix[t - 1, 1]], axis=1)

    @pl.when(x == 0)
    def _():
        ein[...] = jnp.zeros_like(ein)

    @pl.when(x > 0)
    def _():
        to_row(total.at[1], ein, 1, 0, 0).wait_recv()

    @pl.when(x == 1)
    def _():
        enext[...] = mm(split(total[0]), split(ein[...])) + total[1]
        to_row(enext, ein, 3, 0, 0).start()
        to_row(enext, ein, 2, 1, 0).start()

    e_s = split(ein[...])

    def stage(t):
        staged[t] = mm(split(full[t, :, :DK]), e_s) + full[t, :, DK:]

    last = []
    for o in range(1, GROUP):
        p = lax.rem(place + o, GROUP)
        stage(p)
        last.append(shared(src_ref=staged.at[p], dst_ref=arrived.at[own], send_sem=send4.at[o - 1],
                           recv_sem=recv4.at[own], device_id={"seq": base + p}))
        last[-1].start()
    stage(place)
    arrived[own] = staged[place]
    for h in range(heads):
        @pl.when(own != h)
        def _(h=h):
            shared(src_ref=staged.at[0], dst_ref=arrived.at[h], send_sem=send4.at[0], recv_sem=recv4.at[h],
                   device_id={"seq": mirror}).wait_recv()
        cols = slice(h * DK, (h + 1) * DK)
        out[:, cols] = out[:, cols] + mm((rhi[:, cols], rlo[:, cols]), split(arrived[h]))

    for copy in copies + halos + [to_mirror(0), to_mirror(1)] + last:
        copy.wait_send()
    for h in range(heads):
        @pl.when(place != seats[h])
        def _(h=h):
            to_owner(h).wait_send()

    @pl.when(x == 0)
    def _():
        to_row(total.at[1], ein, 1, 0, 0).wait_send()

    @pl.when(x == 1)
    def _():
        to_row(enext, ein, 3, 0, 0).wait_send()
        to_row(enext, ein, 2, 1, 0).wait_send()

    @pl.when(x == 2)
    def _():
        to_row(total, tin, 3, 0, 1).wait_send()


def solution(mesh):
    peers, shards = mesh.shape["head"], mesh.shape["seq"]
    rows_x = shards // ZROW
    assert rows_x == 4 and shards == rows_x * ZROW

    def per_device(hid, proj, q, k, v, cq, ck, cv, scale, bias):
        heads, rows = scale.shape[0], q.shape[0]
        key_heads, blocks = q.shape[1] // DK, rows // C
        assert heads == GROUP and rows == blocks * C
        width = q.shape[1] + k.shape[1] + v.shape[1]
        per = proj.shape[1] // peers
        proj = jnp.transpose(proj)
        vm, smem = pl.BlockSpec(memory_space=pltpu.VMEM), pl.BlockSpec(memory_space=pltpu.SMEM)
        dma, pair, square = pltpu.SemaphoreType.DMA, (2, DK, DV), (C, C)

        def f32(*shape):
            return pltpu.VMEM(shape, F32)

        return pl.pallas_call(
            functools.partial(whole_kernel, peers, heads, rows_x),
            out_shape=jax.ShapeDtypeStruct((rows, heads * DV), F32),
            in_specs=[smem] * 2 + [vm] * 3 + [pl.BlockSpec(memory_space=pltpu.HBM)] * 5,
            out_specs=vm,
            scratch_shapes=[
                *(pltpu.VMEM(a.shape, BF16) for a in (hid, proj, q, k, v)), dma((5,)),
                f32(peers, per, rows), f32(peers - 1, per, rows), pltpu.VMEM((HALO, width), BF16),
                f32(rows + 8, width), f32(*q.shape), f32(*k.shape), f32(*v.shape),
                f32(key_heads, blocks, *square), f32(key_heads, blocks, *square),
                f32(heads, blocks, *square), f32(heads, blocks, C, DK + DV),
                f32(heads, blocks - 1, DK, DK + DV), f32(heads, *pair),
                pltpu.VMEM((rows, heads * DK), BF16), pltpu.VMEM((rows, heads * DK), BF16),
                f32(GROUP, *pair), f32(GROUP - 1, *pair), f32(*pair), f32(*pair), f32(*pair), f32(*pair),
                f32(DK, DV), f32(*pair), f32(DK, DV), f32(GROUP, DK, DK + DV),
                f32(GROUP, DK, DV), f32(GROUP, DK, DV),
                dma((peers - 1,)), dma((peers - 1,)), dma((3,)), dma((3,)),
                dma((heads,)), dma((GROUP,)), dma((2,)), dma((2,)), dma((2,)), dma((2,)),
                dma((GROUP - 1,)), dma((GROUP,)),
            ],
            compiler_params=pltpu.CompilerParams(collective_id=0, has_side_effects=True, vmem_limit_bytes=40 * 1024 * 1024),
            name="delta",
        )(*(pltpu.with_memory_space_constraint(a, pltpu.HBM) for a in (scale, bias, cq, ck, cv, hid, proj, q, k, v)))

    placed = (
        P("seq", "head"), P("head", None), P("seq", "head"), P("seq", "head"), P("seq", "head"),
        P(None, "head"), P(None, "head"), P(None, "head"), P("head"), P("head"),
    )
    return jax.shard_map(per_device, mesh=mesh, in_specs=placed, out_specs=P("seq", "head"), check_vma=False)
```

```python
import functools
import math

import jax
import jax.numpy as jnp
from jax import lax
from jax.experimental import pallas as pl
from jax.experimental.pallas import tpu as pltpu
from jax.sharding import PartitionSpec as P

DK = 128
DV = 128
KCONV = 4
C = 128
ZROW = 8
GROUP = 4
BASE = 8
HALO = 16

MESH = pl.DeviceIdType.MESH
F32 = jnp.float32
BF16 = jnp.bfloat16


def split(a):
    hi = a.astype(BF16)
    return hi, (a - hi.astype(F32)).astype(BF16)


NN = (((1,), (0,)), ((), ()))
NT = (((1,), (1,)), ((), ()))


def mm(a, b, dims=NN):
    dot = functools.partial(lax.dot_general, dimension_numbers=dims, preferred_element_type=F32)
    if dims is NN and a[0].shape[1] == 128:
        pair = jnp.concatenate(a, axis=1)
        hi, lo = (jnp.concatenate([x, x], axis=0) for x in b)
        return dot(pair, hi) + dot(pair, lo)
    return dot(a[0], b[0]) + (dot(a[0], b[1]) + dot(a[1], b[0]))


def iota(shape, axis):
    return lax.broadcasted_iota(jnp.int32, shape, axis)


def silu(u):
    return u / (1.0 + jnp.exp(-u))


def inverses(systems):
    lane, sub = iota((BASE, C), 1), iota((BASE, C), 0)
    group, within = lane // BASE, lane & (BASE - 1)
    solved = []
    for a in systems:
        packed = a[0:BASE, :]
        for j in range(1, C // BASE):
            packed = jnp.where(group == j, a[BASE * j:BASE * (j + 1), :], packed)
        tops = [jnp.where(within[i:i + 8] == sub[i:i + 8], 1.0, 0.0) for i in range(0, BASE, 8)]
        for m in range(BASE - 1):
            row = tops[m // 8][m % 8:m % 8 + 1, :]
            for i in range((m + 1) // 8, BASE // 8):
                factor = jnp.take_along_axis(packed[8 * i:8 * i + 8], (lane[:8] - within[:8]) + m, axis=1)
                tops[i] = tops[i] - factor * row
        t = jnp.concatenate(tops, axis=0)
        solved.append(jnp.concatenate([jnp.where(group == j, t, 0.0) for j in range(C // BASE)], axis=0))
    size = BASE
    while size < C:
        count = C // (2 * size)

        def lower(x):
            return jnp.concatenate([x[(2 * j + 1) * size:(2 * j + 2) * size] for j in range(count)], axis=0)

        def weave(upper, low):
            pieces = []
            for j in range(count):
                pieces.append(upper[2 * j * size:(2 * j + 1) * size])
                pieces.append(low[j * size:(j + 1) * size])
            return jnp.concatenate(pieces, axis=0)

        rows, cols = iota((C // 2, C), 0) // size, iota((C // 2, C), 1) // size
        left = cols == 2 * rows
        parts = [split(t) for t in solved]
        inner = [mm(split(jnp.where(left, lower(a), 0.0)), ts) for a, ts in zip(systems, parts)]
        zeros = jnp.zeros((C, C), F32)
        step = [mm(split(lower(t)), split(weave(zeros, p))) for t, p in zip(solved, inner)]
        solved = [weave(t, lower(t) - y) for t, y in zip(solved, step)]
        size *= 2
    return solved


def wide(ref, *at):
    return jnp.concatenate([ref[(*at, 0)], ref[(*at, 1)]], axis=1)


def then(later_move, later_state, x):
    y = mm(split(later_move), split(x))
    return y[:, :DK], y[:, DK:] + later_state


SEAT = (0, 3, 1, 2)


def owned_at(p):
    return jnp.where(p == 0, 0, jnp.where(p == GROUP - 1, 1, p + 1))


def features_kernel(peers, heads, cq, ck, cv, hid_in, proj_in, q_in, k_in, v_in,
                    g_out, uq, uk, uv, kk, qk,
                    hid, proj, q, k, v, load, part, parts, halo, pad, send, recv, hsend, hrecv):
    seq, head = lax.axis_index("seq"), lax.axis_index("head")
    shards = lax.axis_size("seq")
    after, before = lax.rem(seq + 1, shards), lax.rem(seq + shards - 1, shards)
    rows, wq, wk = q.shape[0], q.shape[1], k.shape[1]
    blocks, key_heads = rows // C, wq // DK
    shared = functools.partial(pltpu.make_async_remote_copy, device_id_type=MESH)

    barrier = pltpu.get_barrier_semaphore()
    for o in range(1, peers):
        pl.semaphore_signal(barrier, inc=1, device_id={"head": lax.rem(head + o, peers)}, device_id_type=MESH)
    others = [after, before]
    for s in others:
        pl.semaphore_signal(barrier, inc=1, device_id={"seq": s}, device_id_type=MESH)

    loads = [pltpu.make_async_copy(src, dst, load.at[i]) for i, (src, dst) in enumerate(
        [(hid_in, hid), (proj_in, proj), (q_in, q), (k_in, k), (v_in, v)])]
    for copy in loads:
        copy.start()
    for copy in loads[:2]:
        copy.wait()
    flat = lax.dot_general(proj[...], hid[...], NT, preferred_element_type=F32)
    per = flat.shape[0] // peers
    for p in range(peers):
        part[p] = flat[p * per:(p + 1) * per, :]
    for copy in loads[2:]:
        copy.wait()
    pl.semaphore_wait(barrier, peers - 1 + len(others))
    copies = []
    for o in range(1, peers):
        to = lax.rem(head + o, peers)
        copies.append(shared(src_ref=part.at[to], dst_ref=parts.at[o - 1], send_sem=send.at[o - 1],
                             recv_sem=recv.at[o - 1], device_id={"head": to}))
    columns = [(q, 0), (k, wq), (v, wq + wk)]
    halos = []
    for i, (src, col) in enumerate(columns):
        halos.append(shared(src_ref=src.at[pl.ds(rows - HALO, HALO)],
                            dst_ref=halo.at[:, pl.ds(col, src.shape[1])],
                            send_sem=hsend.at[i], recv_sem=hrecv.at[i], device_id={"seq": after}))
    for copy in halos + copies:
        copy.start()

    for src, col in columns:
        pad[8:8 + rows, col:col + src.shape[1]] = src[...].astype(F32)

    def conv(b, col, taps, tcol):
        summed = None
        for j in range(KCONV):
            term = taps[j:j + 1, tcol:tcol + DK].astype(F32) * pad[5 + j + b * C:5 + j + (b + 1) * C, col:col + DK]
            summed = term if summed is None else summed + term
        return silu(summed)

    def unit(u, factor):
        return u * (lax.rsqrt(jnp.sum(u * u, axis=-1, keepdims=True) + 1e-06) * factor)

    def features(b):
        at = slice(b * C, (b + 1) * C)
        for n in range(key_heads):
            cols = slice(n * DK, (n + 1) * DK)
            queries = unit(conv(b, n * DK, cq, n * DK), 1.0 / math.sqrt(DK))
            keys = unit(conv(b, wq + n * DK, ck, n * DK), 1.0)
            uq[at, cols], uk[at, cols] = queries, keys
            keys_s = split(keys)
            kk[n, b] = mm(keys_s, keys_s, NT)
            qk[n, b] = mm(split(queries), keys_s, NT)
        for h in range(heads):
            uv[at, h * DV:(h + 1) * DV] = conv(b, wq + wk + h * DV, cv, h * DV)

    for b in range(1, blocks):
        features(b)
    for copy in halos:
        copy.wait_recv()
    pad[0:8, :] = jnp.where(seq == 0, 0.0, halo[HALO - 8:HALO, :].astype(F32))
    features(0)

    g = part[head]
    for o, copy in enumerate(copies):
        copy.wait_recv()
        g = g + parts[o]
    g_out[...] = g
    for copy in copies + halos:
        copy.wait_send()


def scan_kernel(heads, rows_x, scale, bias, g_in, uq, uk, uv, kk, qk, out,
                attend, wu, xs, ms, rhi, rlo,
                gathered, prefix, mine, other, total, tin, ein, begin, enext, full, staged, arrived,
                send1, recv1, send2, recv2, send3, recv3, send4, recv4):
    seq = lax.axis_index("seq")
    z, x = lax.rem(seq, ZROW), seq // ZROW
    half, place = z // GROUP, lax.rem(z, GROUP)
    first_half = half == 0
    base = seq - place
    mirror = x * ZROW + (ZROW - 1 - z)
    own = owned_at(jnp.where(first_half, place, GROUP - 1 - place))
    seats = [jnp.where(first_half, SEAT[h], GROUP - 1 - SEAT[h]) for h in range(heads)]
    key_heads, blocks = kk.shape[0], kk.shape[1]
    group = heads // key_heads
    shared = functools.partial(pltpu.make_async_remote_copy, device_id_type=MESH)

    barrier = pltpu.get_barrier_semaphore()
    others = [mirror]
    others += [base + lax.rem(place + o, GROUP) for o in range(1, GROUP)]
    others += [lax.rem(x + o, rows_x) * ZROW + z for o in range(1, rows_x)]
    for s in others:
        pl.semaphore_signal(barrier, inc=1, device_id={"seq": s}, device_id_type=MESH)
    g = g_in[...]

    r, c = iota((C, C), 0), iota((C, C), 1)
    causal, strict = r >= c, r > c
    decays, rates = [], []
    for h in range(heads):
        u = g[2 * h:2 * h + 1, :] + bias[h]
        e = jnp.exp(-jnp.abs(u))
        w = 1.0 + e
        log1p = jnp.where(w == 1.0, e, jnp.log(w) * (e / jnp.where(w == 1.0, 1.0, w - 1.0)))
        decays.append(-scale[h] * (jnp.maximum(u, 0.0) + log1p))
        rates.append(1.0 / (1.0 + jnp.exp(-g[2 * h + 1:2 * h + 2, :])))
    table = jnp.concatenate(decays + rates, axis=0)
    width = table.shape[0]
    table = jnp.concatenate([table[:, b * C:(b + 1) * C] for b in range(blocks)], axis=0)
    cum = lax.dot_general(table, jnp.where(r <= c, 1.0, 0.0), NN, precision=lax.Precision.HIGHEST,
                          preferred_element_type=F32)
    cum_col, rate_col = jnp.transpose(cum), jnp.transpose(table)

    def decay_row(h, b):
        return cum[b * width + h:b * width + h + 1, :]

    def decay_col(h, b):
        return cum_col[:, b * width + h:b * width + h + 1]

    def maps(n):
        every = [(h, b) for b in range(blocks) for h in range(n * group, (n + 1) * group)]
        cols = slice(n * DK, (n + 1) * DK)
        keys = [uk[b * C:(b + 1) * C, cols] for b in range(blocks)]
        systems, betas = [], []
        for h, b in every:
            gap = decay_col(h, b) - decay_row(h, b)
            decay = jnp.where(causal, jnp.exp(jnp.where(causal, gap, 0.0)), 0.0)
            i = b * width + heads + h
            beta = rate_col[:, i:i + 1]
            attend[h, b] = decay * qk[n, b]
            systems.append(jnp.where(strict, beta * decay * kk[n, b], 0.0))
            betas.append(beta)
        solved = inverses(systems)
        right = []
        for (h, b), beta in zip(every, betas):
            values = uv[b * C:(b + 1) * C, h * DV:(h + 1) * DV]
            right.append(split(jnp.concatenate(
                [(beta * jnp.exp(decay_col(h, b))) * keys[b], beta * values], axis=1)))
        solutions = [mm(split(t), y) for t, y in zip(solved, right)]
        keys_t = [jnp.transpose(y) for y in keys]
        eye = jnp.where(r == c, 1.0, 0.0)
        steps = {}
        for (h, b), y in zip(every, solutions):
            wu[h, b] = y
            last = cum[b * width + h:b * width + h + 1, C - 1:C]
            pair = mm(split(keys_t[b] * jnp.exp(last - decay_row(h, b))), split(y))
            steps[h, b] = (jnp.exp(last) * eye - pair[:, :DK], pair[:, DK:])
        for h in range(n * group, (n + 1) * group):
            now = jnp.concatenate(steps[h, 0], axis=1)
            for b in range(1, blocks):
                xs[h, b - 1] = now
                move, state = then(*steps[h, b], now)
                now = jnp.concatenate([move, state], axis=1)
            ms[h, 0], ms[h, 1] = now[:, :DK], now[:, DK:]

    def to_owner(h):
        return shared(src_ref=ms.at[h], dst_ref=gathered.at[place], send_sem=send1.at[h],
                      recv_sem=recv1.at[place], device_id={"seq": base + seats[h]})

    def hand_over(n):
        for h in range(n * group, (n + 1) * group):
            @pl.when(place != seats[h])
            def _(h=h):
                to_owner(h).start()

            @pl.when(place == seats[h])
            def _(h=h):
                gathered[place] = ms[h]

    def responses(n):
        for h in range(n * group, (n + 1) * group):
            cols = slice(h * DK, (h + 1) * DK)
            for b in range(blocks):
                at = slice(b * C, (b + 1) * C)
                y = wu[h, b]
                queries = jnp.exp(decay_col(h, b)) * uq[at, n * DK:(n + 1) * DK]
                if b == 0:
                    got = mm(split(attend[h, b]), split(y))
                    response, rest = queries - got[:, :DK], got[:, DK:]
                else:
                    now = xs[h, b - 1]
                    z = mm(split(y[:, :DK]), split(now))
                    y = jnp.concatenate([-z[:, :DK], y[:, DK:] - z[:, DK:]], axis=1)
                    got = mm(split(jnp.concatenate([queries, attend[h, b]], axis=1)),
                             split(jnp.concatenate([now, y], axis=0)))
                    response, rest = got[:, :DK], got[:, DK:]
                rhi[at, cols], rlo[at, cols] = split(response)
                out[at, cols] = rest

    maps(0)
    pl.semaphore_wait(barrier, len(others))
    hand_over(0)
    maps(1)
    hand_over(1)
    responses(0)

    def arrive(t):
        @pl.when(place != t)
        def _():
            shared(src_ref=ms.at[0], dst_ref=gathered.at[t], send_sem=send1.at[0], recv_sem=recv1.at[t],
                   device_id={"seq": mirror}).wait_recv()

    arrive(0)
    arrive(1)
    early = jnp.concatenate(then(gathered[1, 0], gathered[1, 1], wide(gathered, 0)), axis=1)
    arrive(2)
    arrive(3)
    late = then(gathered[3, 0], gathered[3, 1], wide(gathered, 2))
    mine[0], mine[1] = then(*late, early)

    def to_mirror(i):
        return shared(src_ref=mine.at[i], dst_ref=other.at[i], send_sem=send2.at[i], recv_sem=recv2.at[i],
                      device_id={"seq": mirror})

    lead = jnp.where(first_half, 1, 0)
    to_mirror(lead).start()
    to_mirror(1 - lead).start()
    prefix[0, 0], prefix[0, 1] = gathered[0, 0], gathered[0, 1]
    prefix[1, 0], prefix[1, 1] = early[:, :DK], early[:, DK:]
    prefix[2, 0], prefix[2, 1] = then(gathered[2, 0], gathered[2, 1], early)
    responses(1)

    @pl.when(first_half)
    def _():
        to_mirror(0).wait_recv()
        y = mm(split(other[0]), split(wide(mine)))
        total[0] = y[:, :DK]
        to_mirror(1).wait_recv()
        total[1] = y[:, DK:] + other[1]

    @pl.when(half == 1)
    def _():
        to_mirror(1).wait_recv()
        total[1] = mm(split(mine[0]), split(other[1])) + mine[1]

    def to_row(src, dst, to, i, arrived_at):
        return shared(src_ref=src, dst_ref=dst, send_sem=send3.at[i], recv_sem=recv3.at[arrived_at],
                      device_id={"seq": to * ZROW + z})

    @pl.when(x == 0)
    def _():
        to_row(total.at[1], ein, 1, 0, 0).start()

    @pl.when(half == 1)
    def _():
        to_mirror(0).wait_recv()
        total[0] = mm(split(mine[0]), split(other[0]))

    @pl.when(x == 2)
    def _():
        to_row(total, tin, 3, 0, 1).start()

    eye = jnp.where(r == c, 1.0, 0.0)
    begin[0] = jnp.where(first_half, eye, other[0])
    begin[1] = jnp.where(first_half, 0.0, other[1])

    @pl.when(x == 3)
    def _():
        to_row(total, tin, 3, 0, 1).wait_recv()
        begin[0], begin[1] = then(begin[0], begin[1], wide(tin))

    start_s = split(wide(begin))
    full[0] = wide(begin)
    for t in range(1, GROUP):
        y = mm(split(prefix[t - 1, 0]), start_s)
        full[t] = jnp.concatenate([y[:, :DK], y[:, DK:] + prefix[t - 1, 1]], axis=1)

    @pl.when(x == 0)
    def _():
        ein[...] = jnp.zeros_like(ein)

    @pl.when(x > 0)
    def _():
        to_row(total.at[1], ein, 1, 0, 0).wait_recv()

    @pl.when(x == 1)
    def _():
        enext[...] = mm(split(total[0]), split(ein[...])) + total[1]
        to_row(enext, ein, 3, 0, 0).start()
        to_row(enext, ein, 2, 1, 0).start()

    e_s = split(ein[...])

    def stage(t):
        staged[t] = mm(split(full[t, :, :DK]), e_s) + full[t, :, DK:]

    last = []
    for o in range(1, GROUP):
        p = lax.rem(place + o, GROUP)
        stage(p)
        last.append(shared(src_ref=staged.at[p], dst_ref=arrived.at[own], send_sem=send4.at[o - 1],
                           recv_sem=recv4.at[own], device_id={"seq": base + p}))
        last[-1].start()
    stage(place)
    arrived[own] = staged[place]
    for h in range(heads):
        @pl.when(own != h)
        def _(h=h):
            shared(src_ref=staged.at[0], dst_ref=arrived.at[h], send_sem=send4.at[0], recv_sem=recv4.at[h],
                   device_id={"seq": mirror}).wait_recv()
        cols = slice(h * DK, (h + 1) * DK)
        out[:, cols] = out[:, cols] + mm((rhi[:, cols], rlo[:, cols]), split(arrived[h]))

    for copy in [to_mirror(0), to_mirror(1)] + last:
        copy.wait_send()
    for h in range(heads):
        @pl.when(place != seats[h])
        def _(h=h):
            to_owner(h).wait_send()

    @pl.when(x == 0)
    def _():
        to_row(total.at[1], ein, 1, 0, 0).wait_send()

    @pl.when(x == 1)
    def _():
        to_row(enext, ein, 3, 0, 0).wait_send()
        to_row(enext, ein, 2, 1, 0).wait_send()

    @pl.when(x == 2)
    def _():
        to_row(total, tin, 3, 0, 1).wait_send()


def solution(mesh):
    peers, shards = mesh.shape["head"], mesh.shape["seq"]
    rows_x = shards // ZROW
    assert rows_x == 4 and shards == rows_x * ZROW

    def per_device(hid, proj, q, k, v, cq, ck, cv, scale, bias):
        heads, rows = scale.shape[0], q.shape[0]
        key_heads, blocks = q.shape[1] // DK, rows // C
        assert heads == GROUP and rows == blocks * C
        width = q.shape[1] + k.shape[1] + v.shape[1]
        per = proj.shape[1] // peers
        proj = jnp.transpose(proj)
        vm, smem = pl.BlockSpec(memory_space=pltpu.VMEM), pl.BlockSpec(memory_space=pltpu.SMEM)
        dma, pair, square = pltpu.SemaphoreType.DMA, (2, DK, DV), (C, C)

        def f32(*shape):
            return pltpu.VMEM(shape, F32)

        def result(*shape):
            return jax.ShapeDtypeStruct(shape, F32)

        def pinned(*arrays):
            return [pltpu.with_memory_space_constraint(a, pltpu.HBM) for a in arrays]

        made = pl.pallas_call(
            functools.partial(features_kernel, peers, heads),
            out_shape=(result(per, rows), result(*q.shape), result(*k.shape), result(*v.shape),
                       result(key_heads, blocks, *square), result(key_heads, blocks, *square)),
            in_specs=[vm] * 3 + [pl.BlockSpec(memory_space=pltpu.HBM)] * 5,
            out_specs=(vm,) * 6,
            scratch_shapes=[
                *(pltpu.VMEM(a.shape, BF16) for a in (hid, proj, q, k, v)), dma((5,)),
                f32(peers, per, rows), f32(peers - 1, per, rows), pltpu.VMEM((HALO, width), BF16),
                f32(rows + 8, width),
                dma((peers - 1,)), dma((peers - 1,)), dma((3,)), dma((3,)),
            ],
            compiler_params=pltpu.CompilerParams(collective_id=0, has_side_effects=True, vmem_limit_bytes=24 * 1024 * 1024),
            name="features",
        )(*pinned(cq, ck, cv, hid, proj, q, k, v))
        return pl.pallas_call(
            functools.partial(scan_kernel, heads, rows_x),
            out_shape=result(rows, heads * DV),
            in_specs=[smem] * 2 + [vm] * 6,
            out_specs=vm,
            scratch_shapes=[
                f32(heads, blocks, *square), f32(heads, blocks, C, DK + DV),
                f32(heads, blocks - 1, DK, DK + DV), f32(heads, *pair),
                pltpu.VMEM((rows, heads * DK), BF16), pltpu.VMEM((rows, heads * DK), BF16),
                f32(GROUP, *pair), f32(GROUP - 1, *pair), f32(*pair), f32(*pair), f32(*pair), f32(*pair),
                f32(DK, DV), f32(*pair), f32(DK, DV), f32(GROUP, DK, DK + DV),
                f32(GROUP, DK, DV), f32(GROUP, DK, DV),
                dma((heads,)), dma((GROUP,)), dma((2,)), dma((2,)), dma((2,)), dma((2,)),
                dma((GROUP - 1,)), dma((GROUP,)),
            ],
            compiler_params=pltpu.CompilerParams(collective_id=1, has_side_effects=True, vmem_limit_bytes=36 * 1024 * 1024),
            name="scan",
        )(*pinned(scale, bias), *made)

    placed = (
        P("seq", "head"), P("head", None), P("seq", "head"), P("seq", "head"), P("seq", "head"),
        P(None, "head"), P(None, "head"), P(None, "head"), P("head"), P("head"),
    )
    return jax.shard_map(per_device, mesh=mesh, in_specs=placed, out_specs=P("seq", "head"), check_vma=False)
```

```python
import functools
import math

import jax
import jax.numpy as jnp
from jax import lax
from jax.experimental import pallas as pl
from jax.experimental.pallas import tpu as pltpu
from jax.sharding import PartitionSpec as P

DK = 128
DV = 128
KCONV = 4
C = 128
ZROW = 8
GROUP = 4
BASE = 8
HALO = 16

MESH = pl.DeviceIdType.MESH
F32 = jnp.float32
BF16 = jnp.bfloat16


def split(a):
    hi = a.astype(BF16)
    return hi, (a - hi.astype(F32)).astype(BF16)


NN = (((1,), (0,)), ((), ()))
NT = (((1,), (1,)), ((), ()))


def mm(a, b, dims=NN):
    dot = functools.partial(lax.dot_general, dimension_numbers=dims, preferred_element_type=F32)
    if dims is NN and a[0].shape[1] == 128:
        pair = jnp.concatenate(a, axis=1)
        hi, lo = (jnp.concatenate([x, x], axis=0) for x in b)
        return dot(pair, hi) + dot(pair, lo)
    return dot(a[0], b[0]) + (dot(a[0], b[1]) + dot(a[1], b[0]))


def iota(shape, axis):
    return lax.broadcasted_iota(jnp.int32, shape, axis)


def silu(u):
    return u / (1.0 + jnp.exp(-u))


def inverses(systems):
    lane, sub = iota((BASE, C), 1), iota((BASE, C), 0)
    group, within = lane // BASE, lane & (BASE - 1)
    solved = []
    for a in systems:
        packed = a[0:BASE, :]
        for j in range(1, C // BASE):
            packed = jnp.where(group == j, a[BASE * j:BASE * (j + 1), :], packed)
        tops = [jnp.where(within[i:i + 8] == sub[i:i + 8], 1.0, 0.0) for i in range(0, BASE, 8)]
        for m in range(BASE - 1):
            row = tops[m // 8][m % 8:m % 8 + 1, :]
            for i in range((m + 1) // 8, BASE // 8):
                factor = jnp.take_along_axis(packed[8 * i:8 * i + 8], (lane[:8] - within[:8]) + m, axis=1)
                tops[i] = tops[i] - factor * row
        t = jnp.concatenate(tops, axis=0)
        solved.append(jnp.concatenate([jnp.where(group == j, t, 0.0) for j in range(C // BASE)], axis=0))
    size = BASE
    while size < C:
        count = C // (2 * size)

        def lower(x):
            return jnp.concatenate([x[(2 * j + 1) * size:(2 * j + 2) * size] for j in range(count)], axis=0)

        def weave(upper, low):
            pieces = []
            for j in range(count):
                pieces.append(upper[2 * j * size:(2 * j + 1) * size])
                pieces.append(low[j * size:(j + 1) * size])
            return jnp.concatenate(pieces, axis=0)

        rows, cols = iota((C // 2, C), 0) // size, iota((C // 2, C), 1) // size
        left = cols == 2 * rows
        parts = [split(t) for t in solved]
        inner = [mm(split(jnp.where(left, lower(a), 0.0)), ts) for a, ts in zip(systems, parts)]
        zeros = jnp.zeros((C, C), F32)
        step = [mm(split(lower(t)), split(weave(zeros, p))) for t, p in zip(solved, inner)]
        solved = [weave(t, lower(t) - y) for t, y in zip(solved, step)]
        size *= 2
    return solved


def wide(ref, *at):
    return jnp.concatenate([ref[(*at, 0)], ref[(*at, 1)]], axis=1)


def then(later_move, later_state, x):
    y = mm(split(later_move), split(x))
    return y[:, :DK], y[:, DK:] + later_state


SEAT = (0, 3, 1, 2)


def owned_at(p):
    return jnp.where(p == 0, 0, jnp.where(p == GROUP - 1, 1, p + 1))


def features_kernel(peers, heads, cq, ck, cv, hid_in, proj_in, q_in, k_in, v_in,
                    g_out, uq, uk, uv, kk, qk,
                    hid, proj, q, k, v, load, part, parts, halo, pad, send, recv, hsend, hrecv):
    seq, head = lax.axis_index("seq"), lax.axis_index("head")
    shards = lax.axis_size("seq")
    after, before = lax.rem(seq + 1, shards), lax.rem(seq + shards - 1, shards)
    rows, wq, wk = q.shape[0], q.shape[1], k.shape[1]
    blocks, key_heads = rows // C, wq // DK
    shared = functools.partial(pltpu.make_async_remote_copy, device_id_type=MESH)

    barrier = pltpu.get_barrier_semaphore()
    for o in range(1, peers):
        pl.semaphore_signal(barrier, inc=1, device_id={"head": lax.rem(head + o, peers)}, device_id_type=MESH)
    others = [after, before]
    for s in others:
        pl.semaphore_signal(barrier, inc=1, device_id={"seq": s}, device_id_type=MESH)

    loads = [pltpu.make_async_copy(src, dst, load.at[i]) for i, (src, dst) in enumerate(
        [(hid_in, hid), (proj_in, proj), (q_in, q), (k_in, k), (v_in, v)])]
    for copy in loads:
        copy.start()
    for copy in loads[:2]:
        copy.wait()
    flat = lax.dot_general(proj[...], hid[...], NT, preferred_element_type=F32)
    per = flat.shape[0] // peers
    for p in range(peers):
        part[p] = flat[p * per:(p + 1) * per, :]
    for copy in loads[2:]:
        copy.wait()
    pl.semaphore_wait(barrier, peers - 1 + len(others))
    copies = []
    for o in range(1, peers):
        to = lax.rem(head + o, peers)
        copies.append(shared(src_ref=part.at[to], dst_ref=parts.at[o - 1], send_sem=send.at[o - 1],
                             recv_sem=recv.at[o - 1], device_id={"head": to}))
    columns = [(q, 0), (k, wq), (v, wq + wk)]
    halos = []
    for i, (src, col) in enumerate(columns):
        halos.append(shared(src_ref=src.at[pl.ds(rows - HALO, HALO)],
                            dst_ref=halo.at[:, pl.ds(col, src.shape[1])],
                            send_sem=hsend.at[i], recv_sem=hrecv.at[i], device_id={"seq": after}))
    for copy in halos + copies:
        copy.start()

    for src, col in columns:
        pad[8:8 + rows, col:col + src.shape[1]] = src[...].astype(F32)

    def conv(b, col, taps, tcol):
        summed = None
        for j in range(KCONV):
            term = taps[j:j + 1, tcol:tcol + DK].astype(F32) * pad[5 + j + b * C:5 + j + (b + 1) * C, col:col + DK]
            summed = term if summed is None else summed + term
        return silu(summed)

    def unit(u, factor):
        return u * (lax.rsqrt(jnp.sum(u * u, axis=-1, keepdims=True) + 1e-06) * factor)

    def features(b):
        at = slice(b * C, (b + 1) * C)
        for n in range(key_heads):
            cols = slice(n * DK, (n + 1) * DK)
            queries = unit(conv(b, n * DK, cq, n * DK), 1.0 / math.sqrt(DK))
            keys = unit(conv(b, wq + n * DK, ck, n * DK), 1.0)
            uq[at, cols], uk[at, cols] = queries, keys
            keys_s = split(keys)
            kk[n, b] = mm(keys_s, keys_s, NT)
            qk[n, b] = mm(split(queries), keys_s, NT)
        for h in range(heads):
            uv[at, h * DV:(h + 1) * DV] = conv(b, wq + wk + h * DV, cv, h * DV)

    for b in range(1, blocks):
        features(b)
    for copy in halos:
        copy.wait_recv()
    pad[0:8, :] = jnp.where(seq == 0, 0.0, halo[HALO - 8:HALO, :].astype(F32))
    features(0)

    g = part[head]
    for o, copy in enumerate(copies):
        copy.wait_recv()
        g = g + parts[o]
    g_out[...] = g
    for copy in copies + halos:
        copy.wait_send()


def scan_kernel(heads, rows_x, scale, bias, g_in, uq, uk, uv, kk, qk, out,
                attend, wu, xs, third, ms, rhi, rlo,
                gathered, prefix, mine, other, total, tin, ein, begin, enext, full, fhi, flo, staged, arrived,
                send1, recv1, send2, recv2, send3, recv3, send4, recv4):
    seq = lax.axis_index("seq")
    z, x = lax.rem(seq, ZROW), seq // ZROW
    half, place = z // GROUP, lax.rem(z, GROUP)
    first_half = half == 0
    base = seq - place
    mirror = x * ZROW + (ZROW - 1 - z)
    own = owned_at(jnp.where(first_half, place, GROUP - 1 - place))
    seats = [jnp.where(first_half, SEAT[h], GROUP - 1 - SEAT[h]) for h in range(heads)]
    key_heads, blocks = kk.shape[0], kk.shape[1]
    group = heads // key_heads
    shared = functools.partial(pltpu.make_async_remote_copy, device_id_type=MESH)

    barrier = pltpu.get_barrier_semaphore()
    others = [mirror]
    others += [base + lax.rem(place + o, GROUP) for o in range(1, GROUP)]
    others += [lax.rem(x + o, rows_x) * ZROW + z for o in range(1, rows_x)]
    for s in others:
        pl.semaphore_signal(barrier, inc=1, device_id={"seq": s}, device_id_type=MESH)
    g = g_in[...]

    r, c = iota((C, C), 0), iota((C, C), 1)
    causal, strict = r >= c, r > c
    decays, rates = [], []
    for h in range(heads):
        u = g[2 * h:2 * h + 1, :] + bias[h]
        e = jnp.exp(-jnp.abs(u))
        w = 1.0 + e
        log1p = jnp.where(w == 1.0, e, jnp.log(w) * (e / jnp.where(w == 1.0, 1.0, w - 1.0)))
        decays.append(-scale[h] * (jnp.maximum(u, 0.0) + log1p))
        rates.append(1.0 / (1.0 + jnp.exp(-g[2 * h + 1:2 * h + 2, :])))
    table = jnp.concatenate(decays + rates, axis=0)
    width = table.shape[0]
    table = jnp.concatenate([table[:, b * C:(b + 1) * C] for b in range(blocks)], axis=0)
    cum = lax.dot_general(table, jnp.where(r <= c, 1.0, 0.0), NN, precision=lax.Precision.HIGHEST,
                          preferred_element_type=F32)
    cum_col, rate_col = jnp.transpose(cum), jnp.transpose(table)

    def decay_row(h, b):
        return cum[b * width + h:b * width + h + 1, :]

    def decay_col(h, b):
        return cum_col[:, b * width + h:b * width + h + 1]

    def maps(n):
        every = [(h, b) for b in range(blocks) for h in range(n * group, (n + 1) * group)]
        cols = slice(n * DK, (n + 1) * DK)
        keys = [uk[b * C:(b + 1) * C, cols] for b in range(blocks)]
        systems, betas = [], []
        for h, b in every:
            gap = decay_col(h, b) - decay_row(h, b)
            decay = jnp.where(causal, jnp.exp(jnp.where(causal, gap, 0.0)), 0.0)
            i = b * width + heads + h
            beta = rate_col[:, i:i + 1]
            attend[h, b] = decay * qk[n, b]
            systems.append(jnp.where(strict, beta * decay * kk[n, b], 0.0))
            betas.append(beta)
        solved = inverses(systems)
        right = []
        for (h, b), beta in zip(every, betas):
            values = uv[b * C:(b + 1) * C, h * DV:(h + 1) * DV]
            right.append(split(jnp.concatenate(
                [(beta * jnp.exp(decay_col(h, b))) * keys[b], beta * values], axis=1)))
        solutions = [mm(split(t), y) for t, y in zip(solved, right)]
        keys_t = [jnp.transpose(y) for y in keys]
        eye = jnp.where(r == c, 1.0, 0.0)
        steps = {}
        for (h, b), y in zip(every, solutions):
            wu[h, b] = y
            last = cum[b * width + h:b * width + h + 1, C - 1:C]
            pair = mm(split(keys_t[b] * jnp.exp(last - decay_row(h, b))), split(y))
            steps[h, b] = (jnp.exp(last) * eye - pair[:, :DK], pair[:, DK:])
        mine_now = range(n * group, (n + 1) * group)
        for level in range(blocks // 2):
            pair = {}
            for h in mine_now:
                b = 2 * level
                now = jnp.concatenate(steps[h, b], axis=1)
                pair[h] = then(*steps[h, b + 1], now)
                if level == 0:
                    xs[h, 0], xs[h, 1] = now, jnp.concatenate(pair[h], axis=1)
                else:
                    third[h] = now
            tops = pair if level == 0 else {h: then(*pair[h], jnp.concatenate(tops[h], axis=1)) for h in mine_now}
        for h in mine_now:
            ms[h, 0], ms[h, 1] = tops[h]

    def to_owner(h):
        return shared(src_ref=ms.at[h], dst_ref=gathered.at[place], send_sem=send1.at[h],
                      recv_sem=recv1.at[place], device_id={"seq": base + seats[h]})

    def hand_over(n):
        for h in range(n * group, (n + 1) * group):
            @pl.when(place != seats[h])
            def _(h=h):
                to_owner(h).start()

            @pl.when(place == seats[h])
            def _(h=h):
                gathered[place] = ms[h]

    def responses(n):
        for h in range(n * group, (n + 1) * group):
            cols = slice(h * DK, (h + 1) * DK)
            for b in range(blocks):
                at = slice(b * C, (b + 1) * C)
                y = wu[h, b]
                queries = jnp.exp(decay_col(h, b)) * uq[at, n * DK:(n + 1) * DK]
                if b == 0:
                    got = mm(split(attend[h, b]), split(y))
                    response, rest = queries - got[:, :DK], got[:, DK:]
                else:
                    if b < blocks - 1:
                        now = xs[h, b - 1]
                    else:
                        now = third[h]
                        now = jnp.concatenate(then(now[:, :DK], now[:, DK:], xs[h, b - 2]), axis=1)
                    z = mm(split(y[:, :DK]), split(now))
                    y = jnp.concatenate([-z[:, :DK], y[:, DK:] - z[:, DK:]], axis=1)
                    got = mm(split(jnp.concatenate([queries, attend[h, b]], axis=1)),
                             split(jnp.concatenate([now, y], axis=0)))
                    response, rest = got[:, :DK], got[:, DK:]
                rhi[at, cols], rlo[at, cols] = split(response)
                out[at, cols] = rest

    maps(0)
    pl.semaphore_wait(barrier, len(others))
    hand_over(0)
    maps(1)
    hand_over(1)
    responses(0)

    def arrive(t):
        @pl.when(place != t)
        def _():
            shared(src_ref=ms.at[0], dst_ref=gathered.at[t], send_sem=send1.at[0], recv_sem=recv1.at[t],
                   device_id={"seq": mirror}).wait_recv()

    arrive(0)
    arrive(1)
    early = jnp.concatenate(then(gathered[1, 0], gathered[1, 1], wide(gathered, 0)), axis=1)
    arrive(2)
    arrive(3)
    late = then(gathered[3, 0], gathered[3, 1], wide(gathered, 2))
    mine[0], mine[1] = then(*late, early)

    def to_mirror(i):
        return shared(src_ref=mine.at[i], dst_ref=other.at[i], send_sem=send2.at[i], recv_sem=recv2.at[i],
                      device_id={"seq": mirror})

    lead = jnp.where(first_half, 1, 0)
    to_mirror(lead).start()
    to_mirror(1 - lead).start()
    prefix[0, 0], prefix[0, 1] = gathered[0, 0], gathered[0, 1]
    prefix[1, 0], prefix[1, 1] = early[:, :DK], early[:, DK:]
    prefix[2, 0], prefix[2, 1] = then(gathered[2, 0], gathered[2, 1], early)
    responses(1)

    @pl.when(first_half)
    def _():
        to_mirror(0).wait_recv()
        y = mm(split(other[0]), split(wide(mine)))
        total[0] = y[:, :DK]
        to_mirror(1).wait_recv()
        total[1] = y[:, DK:] + other[1]

    @pl.when(half == 1)
    def _():
        to_mirror(1).wait_recv()
        total[1] = mm(split(mine[0]), split(other[1])) + mine[1]

    def to_row(src, dst, to, i, arrived_at):
        return shared(src_ref=src, dst_ref=dst, send_sem=send3.at[i], recv_sem=recv3.at[arrived_at],
                      device_id={"seq": to * ZROW + z})

    @pl.when(x == 0)
    def _():
        to_row(total.at[1], ein, 1, 0, 0).start()

    @pl.when(half == 1)
    def _():
        to_mirror(0).wait_recv()
        total[0] = mm(split(mine[0]), split(other[0]))

    @pl.when(x == 2)
    def _():
        to_row(total, tin, 3, 0, 1).start()

    eye = jnp.where(r == c, 1.0, 0.0)
    begin[0] = jnp.where(first_half, eye, other[0])
    begin[1] = jnp.where(first_half, 0.0, other[1])

    @pl.when(x == 3)
    def _():
        to_row(total, tin, 3, 0, 1).wait_recv()
        begin[0], begin[1] = then(begin[0], begin[1], wide(tin))

    start_s = split(wide(begin))
    fhi[0:DK, :], flo[0:DK, :] = start_s[0][:, :DK], start_s[1][:, :DK]
    full[0:DK, :] = begin[1]
    for t in range(1, GROUP):
        y = mm(split(prefix[t - 1, 0]), start_s)
        at = slice(t * DK, (t + 1) * DK)
        fhi[at, :], flo[at, :] = split(y[:, :DK])
        full[at, :] = y[:, DK:] + prefix[t - 1, 1]

    @pl.when(x == 0)
    def _():
        ein[...] = jnp.zeros_like(ein)

    @pl.when(x > 0)
    def _():
        to_row(total.at[1], ein, 1, 0, 0).wait_recv()

    @pl.when(x == 1)
    def _():
        enext[...] = mm(split(total[0]), split(ein[...])) + total[1]
        to_row(enext, ein, 3, 0, 0).start()
        to_row(enext, ein, 2, 1, 0).start()

    e_s = split(ein[...])

    y = mm((fhi[...], flo[...]), e_s) + full[...]
    for t in range(GROUP):
        staged[t] = y[t * DK:(t + 1) * DK]
    last = []
    for o in range(1, GROUP):
        p = lax.rem(place + o, GROUP)
        last.append(shared(src_ref=staged.at[p], dst_ref=arrived.at[own], send_sem=send4.at[o - 1],
                           recv_sem=recv4.at[own], device_id={"seq": base + p}))
        last[-1].start()
    arrived[own] = staged[place]
    for h in range(heads):
        @pl.when(own != h)
        def _(h=h):
            shared(src_ref=staged.at[0], dst_ref=arrived.at[h], send_sem=send4.at[0], recv_sem=recv4.at[h],
                   device_id={"seq": mirror}).wait_recv()
        cols = slice(h * DK, (h + 1) * DK)
        out[:, cols] = out[:, cols] + mm((rhi[:, cols], rlo[:, cols]), split(arrived[h]))

    for copy in [to_mirror(0), to_mirror(1)] + last:
        copy.wait_send()
    for h in range(heads):
        @pl.when(place != seats[h])
        def _(h=h):
            to_owner(h).wait_send()

    @pl.when(x == 0)
    def _():
        to_row(total.at[1], ein, 1, 0, 0).wait_send()

    @pl.when(x == 1)
    def _():
        to_row(enext, ein, 3, 0, 0).wait_send()
        to_row(enext, ein, 2, 1, 0).wait_send()

    @pl.when(x == 2)
    def _():
        to_row(total, tin, 3, 0, 1).wait_send()


def solution(mesh):
    peers, shards = mesh.shape["head"], mesh.shape["seq"]
    rows_x = shards // ZROW
    assert rows_x == 4 and shards == rows_x * ZROW

    def per_device(hid, proj, q, k, v, cq, ck, cv, scale, bias):
        heads, rows = scale.shape[0], q.shape[0]
        key_heads, blocks = q.shape[1] // DK, rows // C
        assert heads == GROUP and blocks == 4 and rows == blocks * C
        width = q.shape[1] + k.shape[1] + v.shape[1]
        per = proj.shape[1] // peers
        proj = jnp.transpose(proj)
        vm, smem = pl.BlockSpec(memory_space=pltpu.VMEM), pl.BlockSpec(memory_space=pltpu.SMEM)
        dma, pair, square = pltpu.SemaphoreType.DMA, (2, DK, DV), (C, C)

        def f32(*shape):
            return pltpu.VMEM(shape, F32)

        def result(*shape):
            return jax.ShapeDtypeStruct(shape, F32)

        def pinned(*arrays):
            return [pltpu.with_memory_space_constraint(a, pltpu.HBM) for a in arrays]

        made = pl.pallas_call(
            functools.partial(features_kernel, peers, heads),
            out_shape=(result(per, rows), result(*q.shape), result(*k.shape), result(*v.shape),
                       result(key_heads, blocks, *square), result(key_heads, blocks, *square)),
            in_specs=[vm] * 3 + [pl.BlockSpec(memory_space=pltpu.HBM)] * 5,
            out_specs=(vm,) * 6,
            scratch_shapes=[
                *(pltpu.VMEM(a.shape, BF16) for a in (hid, proj, q, k, v)), dma((5,)),
                f32(peers, per, rows), f32(peers - 1, per, rows), pltpu.VMEM((HALO, width), BF16),
                f32(rows + 8, width),
                dma((peers - 1,)), dma((peers - 1,)), dma((3,)), dma((3,)),
            ],
            compiler_params=pltpu.CompilerParams(collective_id=0, has_side_effects=True, vmem_limit_bytes=24 * 1024 * 1024),
            name="features",
        )(*pinned(cq, ck, cv, hid, proj, q, k, v))
        return pl.pallas_call(
            functools.partial(scan_kernel, heads, rows_x),
            out_shape=result(rows, heads * DV),
            in_specs=[smem] * 2 + [vm] * 6,
            out_specs=vm,
            scratch_shapes=[
                f32(heads, blocks, *square), f32(heads, blocks, C, DK + DV),
                f32(heads, blocks - 2, DK, DK + DV), f32(heads, DK, DK + DV), f32(heads, *pair),
                pltpu.VMEM((rows, heads * DK), BF16), pltpu.VMEM((rows, heads * DK), BF16),
                f32(GROUP, *pair), f32(GROUP - 1, *pair), f32(*pair), f32(*pair), f32(*pair), f32(*pair),
                f32(DK, DV), f32(*pair), f32(DK, DV), f32(GROUP * DK, DV),
                pltpu.VMEM((GROUP * DK, DK), BF16), pltpu.VMEM((GROUP * DK, DK), BF16),
                f32(GROUP, DK, DV), f32(GROUP, DK, DV),
                dma((heads,)), dma((GROUP,)), dma((2,)), dma((2,)), dma((2,)), dma((2,)),
                dma((GROUP - 1,)), dma((GROUP,)),
            ],
            compiler_params=pltpu.CompilerParams(collective_id=1, has_side_effects=True, vmem_limit_bytes=36 * 1024 * 1024),
            name="scan",
        )(*pinned(scale, bias), *made)

    placed = (
        P("seq", "head"), P("head", None), P("seq", "head"), P("seq", "head"), P("seq", "head"),
        P(None, "head"), P(None, "head"), P(None, "head"), P("head"), P("head"),
    )
    return jax.shard_map(per_device, mesh=mesh, in_specs=placed, out_specs=P("seq", "head"), check_vma=False)
```

```python
import functools
import math

import jax
import jax.numpy as jnp
from jax import lax
from jax.experimental import pallas as pl
from jax.experimental.pallas import tpu as pltpu
from jax.sharding import PartitionSpec as P

DK = 128
DV = 128
KCONV = 4
C = 128
ZROW = 8
GROUP = 4
BASE = 8
HALO = 16

MESH = pl.DeviceIdType.MESH
F32 = jnp.float32
BF16 = jnp.bfloat16


def split(a):
    hi = a.astype(BF16)
    return hi, (a - hi.astype(F32)).astype(BF16)


NN = (((1,), (0,)), ((), ()))
NT = (((1,), (1,)), ((), ()))


def mm(a, b, dims=NN):
    dot = functools.partial(lax.dot_general, dimension_numbers=dims, preferred_element_type=F32)
    if dims is NN and a[0].shape[1] == 128:
        pair = jnp.concatenate(a, axis=1)
        hi, lo = (jnp.concatenate([x, x], axis=0) for x in b)
        return dot(pair, hi) + dot(pair, lo)
    return dot(a[0], b[0]) + (dot(a[0], b[1]) + dot(a[1], b[0]))


def iota(shape, axis):
    return lax.broadcasted_iota(jnp.int32, shape, axis)


def silu(u):
    return u / (1.0 + jnp.exp(-u))


def inverses(systems):
    lane, sub = iota((BASE, C), 1), iota((BASE, C), 0)
    group, within = lane // BASE, lane & (BASE - 1)
    solved = []
    for a in systems:
        packed = a[0:BASE, :]
        for j in range(1, C // BASE):
            packed = jnp.where(group == j, a[BASE * j:BASE * (j + 1), :], packed)
        tops = [jnp.where(within[i:i + 8] == sub[i:i + 8], 1.0, 0.0) for i in range(0, BASE, 8)]
        for m in range(BASE - 1):
            row = tops[m // 8][m % 8:m % 8 + 1, :]
            for i in range((m + 1) // 8, BASE // 8):
                factor = jnp.take_along_axis(packed[8 * i:8 * i + 8], (lane[:8] - within[:8]) + m, axis=1)
                tops[i] = tops[i] - factor * row
        t = jnp.concatenate(tops, axis=0)
        solved.append(jnp.concatenate([jnp.where(group == j, t, 0.0) for j in range(C // BASE)], axis=0))
    size = BASE
    while size < C:
        count = C // (2 * size)

        def lower(x):
            return jnp.concatenate([x[(2 * j + 1) * size:(2 * j + 2) * size] for j in range(count)], axis=0)

        def weave(upper, low):
            pieces = []
            for j in range(count):
                pieces.append(upper[2 * j * size:(2 * j + 1) * size])
                pieces.append(low[j * size:(j + 1) * size])
            return jnp.concatenate(pieces, axis=0)

        rows, cols = iota((C // 2, C), 0) // size, iota((C // 2, C), 1) // size
        left = cols == 2 * rows
        parts = [split(t) for t in solved]
        inner = [mm(split(jnp.where(left, lower(a), 0.0)), ts) for a, ts in zip(systems, parts)]
        zeros = jnp.zeros((C, C), F32)
        step = [mm(split(lower(t)), split(weave(zeros, p))) for t, p in zip(solved, inner)]
        solved = [weave(t, lower(t) - y) for t, y in zip(solved, step)]
        size *= 2
    return solved


def wide(ref, *at):
    return jnp.concatenate([ref[(*at, 0)], ref[(*at, 1)]], axis=1)


def then(later_move, later_state, x):
    y = mm(split(later_move), split(x))
    return y[:, :DK], y[:, DK:] + later_state


SEAT = (0, 3, 1, 2)


def owned_at(p):
    return jnp.where(p == 0, 0, jnp.where(p == GROUP - 1, 1, p + 1))


def features_kernel(peers, heads, cq, ck, cv, hid_in, proj_in, q_in, k_in, v_in,
                    g_out, uq, uk, uv, kk, qk,
                    hid, proj, q, k, v, load, part, parts, halo, pad, send, recv, hsend, hrecv):
    seq, head = lax.axis_index("seq"), lax.axis_index("head")
    shards = lax.axis_size("seq")
    after, before = lax.rem(seq + 1, shards), lax.rem(seq + shards - 1, shards)
    rows, wq, wk = q.shape[0], q.shape[1], k.shape[1]
    blocks, key_heads = rows // C, wq // DK
    shared = functools.partial(pltpu.make_async_remote_copy, device_id_type=MESH)

    barrier = pltpu.get_barrier_semaphore()
    for o in range(1, peers):
        pl.semaphore_signal(barrier, inc=1, device_id={"head": lax.rem(head + o, peers)}, device_id_type=MESH)
    others = [after, before]
    for s in others:
        pl.semaphore_signal(barrier, inc=1, device_id={"seq": s}, device_id_type=MESH)

    loads = [pltpu.make_async_copy(src, dst, load.at[i]) for i, (src, dst) in enumerate(
        [(hid_in, hid), (proj_in, proj), (q_in, q), (k_in, k), (v_in, v)])]
    for copy in loads:
        copy.start()
    for copy in loads[:2]:
        copy.wait()
    flat = lax.dot_general(proj[...], hid[...], NT, preferred_element_type=F32)
    per = flat.shape[0] // peers
    for p in range(peers):
        part[p] = flat[p * per:(p + 1) * per, :]
    for copy in loads[2:]:
        copy.wait()
    pl.semaphore_wait(barrier, peers - 1 + len(others))
    copies = []
    for o in range(1, peers):
        to = lax.rem(head + o, peers)
        copies.append(shared(src_ref=part.at[to], dst_ref=parts.at[o - 1], send_sem=send.at[o - 1],
                             recv_sem=recv.at[o - 1], device_id={"head": to}))
    columns = [(q, 0), (k, wq), (v, wq + wk)]
    halos = []
    for i, (src, col) in enumerate(columns):
        halos.append(shared(src_ref=src.at[pl.ds(rows - HALO, HALO)],
                            dst_ref=halo.at[:, pl.ds(col, src.shape[1])],
                            send_sem=hsend.at[i], recv_sem=hrecv.at[i], device_id={"seq": after}))
    for copy in [copies[i] for i in (3, 2, 4, 1, 5, 0, 6)] + halos:
        copy.start()

    for src, col in columns:
        pad[8:8 + rows, col:col + src.shape[1]] = src[...].astype(F32)

    def conv(b, col, taps, tcol):
        summed = None
        for j in range(KCONV):
            term = taps[j:j + 1, tcol:tcol + DK].astype(F32) * pad[5 + j + b * C:5 + j + (b + 1) * C, col:col + DK]
            summed = term if summed is None else summed + term
        return silu(summed)

    def unit(u, factor):
        return u * (lax.rsqrt(jnp.sum(u * u, axis=-1, keepdims=True) + 1e-06) * factor)

    def features(b):
        at = slice(b * C, (b + 1) * C)
        for n in range(key_heads):
            cols = slice(n * DK, (n + 1) * DK)
            queries = unit(conv(b, n * DK, cq, n * DK), 1.0 / math.sqrt(DK))
            keys = unit(conv(b, wq + n * DK, ck, n * DK), 1.0)
            uq[at, cols], uk[at, cols] = queries, keys
            keys_s = split(keys)
            kk[n, b] = mm(keys_s, keys_s, NT)
            qk[n, b] = mm(split(queries), keys_s, NT)
        for h in range(heads):
            uv[at, h * DV:(h + 1) * DV] = conv(b, wq + wk + h * DV, cv, h * DV)

    for b in range(1, blocks):
        features(b)
    for copy in halos:
        copy.wait_recv()
    pad[0:8, :] = jnp.where(seq == 0, 0.0, halo[HALO - 8:HALO, :].astype(F32))
    features(0)

    g = part[head]
    for o, copy in enumerate(copies):
        copy.wait_recv()
        g = g + parts[o]
    g_out[...] = g
    for copy in copies + halos:
        copy.wait_send()


def scan_kernel(heads, rows_x, scale, bias, g_in, uq, uk, uv, kk, qk, out,
                attend, wu, xs, third, ms, rhi, rlo,
                gathered, prefix, mine, other, total, tin, ein, begin, enext, full, fhi, flo, staged, arrived,
                send1, recv1, send2, recv2, send3, recv3, send4, recv4):
    seq = lax.axis_index("seq")
    z, x = lax.rem(seq, ZROW), seq // ZROW
    half, place = z // GROUP, lax.rem(z, GROUP)
    first_half = half == 0
    base = seq - place
    mirror = x * ZROW + (ZROW - 1 - z)
    own = owned_at(jnp.where(first_half, place, GROUP - 1 - place))
    seats = [jnp.where(first_half, SEAT[h], GROUP - 1 - SEAT[h]) for h in range(heads)]
    key_heads, blocks = kk.shape[0], kk.shape[1]
    group = heads // key_heads
    shared = functools.partial(pltpu.make_async_remote_copy, device_id_type=MESH)

    barrier = pltpu.get_barrier_semaphore()
    others = [mirror]
    others += [base + lax.rem(place + o, GROUP) for o in range(1, GROUP)]
    others += [lax.rem(x + o, rows_x) * ZROW + z for o in range(1, rows_x)]
    for s in others:
        pl.semaphore_signal(barrier, inc=1, device_id={"seq": s}, device_id_type=MESH)
    g = g_in[...]

    r, c = iota((C, C), 0), iota((C, C), 1)
    causal, strict = r >= c, r > c
    decays, rates = [], []
    for h in range(heads):
        u = g[2 * h:2 * h + 1, :] + bias[h]
        e = jnp.exp(-jnp.abs(u))
        w = 1.0 + e
        log1p = jnp.where(w == 1.0, e, jnp.log(w) * (e / jnp.where(w == 1.0, 1.0, w - 1.0)))
        decays.append(-scale[h] * (jnp.maximum(u, 0.0) + log1p))
        rates.append(1.0 / (1.0 + jnp.exp(-g[2 * h + 1:2 * h + 2, :])))
    table = jnp.concatenate(decays + rates, axis=0)
    width = table.shape[0]
    table = jnp.concatenate([table[:, b * C:(b + 1) * C] for b in range(blocks)], axis=0)
    cum = lax.dot_general(table, jnp.where(r <= c, 1.0, 0.0), NN, precision=lax.Precision.HIGHEST,
                          preferred_element_type=F32)
    cum_col, rate_col = jnp.transpose(cum), jnp.transpose(table)

    def decay_row(h, b):
        return cum[b * width + h:b * width + h + 1, :]

    def decay_col(h, b):
        return cum_col[:, b * width + h:b * width + h + 1]

    def maps(n):
        every = [(h, b) for b in range(blocks) for h in range(n * group, (n + 1) * group)]
        cols = slice(n * DK, (n + 1) * DK)
        keys = [uk[b * C:(b + 1) * C, cols] for b in range(blocks)]
        systems, betas = [], []
        for h, b in every:
            gap = decay_col(h, b) - decay_row(h, b)
            decay = jnp.where(causal, jnp.exp(jnp.where(causal, gap, 0.0)), 0.0)
            i = b * width + heads + h
            beta = rate_col[:, i:i + 1]
            attend[h, b] = decay * qk[n, b]
            systems.append(jnp.where(strict, beta * decay * kk[n, b], 0.0))
            betas.append(beta)
        solved = inverses(systems)
        right = []
        for (h, b), beta in zip(every, betas):
            values = uv[b * C:(b + 1) * C, h * DV:(h + 1) * DV]
            right.append(split(jnp.concatenate(
                [(beta * jnp.exp(decay_col(h, b))) * keys[b], beta * values], axis=1)))
        solutions = [mm(split(t), y) for t, y in zip(solved, right)]
        keys_t = [jnp.transpose(y) for y in keys]
        eye = jnp.where(r == c, 1.0, 0.0)
        steps = {}
        for (h, b), y in zip(every, solutions):
            wu[h, b] = y
            last = cum[b * width + h:b * width + h + 1, C - 1:C]
            pair = mm(split(keys_t[b] * jnp.exp(last - decay_row(h, b))), split(y))
            steps[h, b] = (jnp.exp(last) * eye - pair[:, :DK], pair[:, DK:])
        mine_now = range(n * group, (n + 1) * group)
        for level in range(blocks // 2):
            pair = {}
            for h in mine_now:
                b = 2 * level
                now = jnp.concatenate(steps[h, b], axis=1)
                pair[h] = then(*steps[h, b + 1], now)
                if level == 0:
                    xs[h, 0], xs[h, 1] = now, jnp.concatenate(pair[h], axis=1)
                else:
                    third[h] = now
            tops = pair if level == 0 else {h: then(*pair[h], jnp.concatenate(tops[h], axis=1)) for h in mine_now}
        for h in mine_now:
            ms[h, 0], ms[h, 1] = tops[h]

    def to_owner(h):
        return shared(src_ref=ms.at[h], dst_ref=gathered.at[place], send_sem=send1.at[h],
                      recv_sem=recv1.at[place], device_id={"seq": base + seats[h]})

    def hand_over(n):
        for h in range(n * group, (n + 1) * group):
            @pl.when(place != seats[h])
            def _(h=h):
                to_owner(h).start()

            @pl.when(place == seats[h])
            def _(h=h):
                gathered[place] = ms[h]

    def responses(n):
        for h in range(n * group, (n + 1) * group):
            cols = slice(h * DK, (h + 1) * DK)
            for b in range(blocks):
                at = slice(b * C, (b + 1) * C)
                y = wu[h, b]
                queries = jnp.exp(decay_col(h, b)) * uq[at, n * DK:(n + 1) * DK]
                if b == 0:
                    got = mm(split(attend[h, b]), split(y))
                    response, rest = queries - got[:, :DK], got[:, DK:]
                else:
                    if b < blocks - 1:
                        now = xs[h, b - 1]
                    else:
                        now = third[h]
                        now = jnp.concatenate(then(now[:, :DK], now[:, DK:], xs[h, b - 2]), axis=1)
                    z = mm(split(y[:, :DK]), split(now))
                    y = jnp.concatenate([-z[:, :DK], y[:, DK:] - z[:, DK:]], axis=1)
                    got = mm(split(jnp.concatenate([queries, attend[h, b]], axis=1)),
                             split(jnp.concatenate([now, y], axis=0)))
                    response, rest = got[:, :DK], got[:, DK:]
                rhi[at, cols], rlo[at, cols] = split(response)
                out[at, cols] = rest

    maps(0)
    pl.semaphore_wait(barrier, len(others))
    hand_over(0)
    maps(1)
    hand_over(1)
    responses(0)

    def arrive(t):
        @pl.when(place != t)
        def _():
            shared(src_ref=ms.at[0], dst_ref=gathered.at[t], send_sem=send1.at[0], recv_sem=recv1.at[t],
                   device_id={"seq": mirror}).wait_recv()

    arrive(0)
    arrive(1)
    early = jnp.concatenate(then(gathered[1, 0], gathered[1, 1], wide(gathered, 0)), axis=1)
    arrive(2)
    arrive(3)
    late = then(gathered[3, 0], gathered[3, 1], wide(gathered, 2))
    mine[0], mine[1] = then(*late, early)

    def to_mirror(i):
        return shared(src_ref=mine.at[i], dst_ref=other.at[i], send_sem=send2.at[i], recv_sem=recv2.at[i],
                      device_id={"seq": mirror})

    lead = jnp.where(first_half, 1, 0)
    to_mirror(lead).start()
    to_mirror(1 - lead).start()
    prefix[0, 0], prefix[0, 1] = gathered[0, 0], gathered[0, 1]
    prefix[1, 0], prefix[1, 1] = early[:, :DK], early[:, DK:]
    prefix[2, 0], prefix[2, 1] = then(gathered[2, 0], gathered[2, 1], early)

    @pl.when(first_half)
    def _():
        to_mirror(0).wait_recv()
        y = mm(split(other[0]), split(wide(mine)))
        total[0] = y[:, :DK]
        to_mirror(1).wait_recv()
        total[1] = y[:, DK:] + other[1]

    @pl.when(half == 1)
    def _():
        to_mirror(1).wait_recv()
        total[1] = mm(split(mine[0]), split(other[1])) + mine[1]

    def to_row(src, dst, to, i, arrived_at):
        return shared(src_ref=src, dst_ref=dst, send_sem=send3.at[i], recv_sem=recv3.at[arrived_at],
                      device_id={"seq": to * ZROW + z})

    @pl.when(x == 0)
    def _():
        to_row(total.at[1], ein, 1, 0, 0).start()

    @pl.when(half == 1)
    def _():
        to_mirror(0).wait_recv()
        total[0] = mm(split(mine[0]), split(other[0]))

    @pl.when(x == 2)
    def _():
        to_row(total, tin, 3, 0, 1).start()

    eye = jnp.where(r == c, 1.0, 0.0)
    begin[0] = jnp.where(first_half, eye, other[0])
    begin[1] = jnp.where(first_half, 0.0, other[1])

    @pl.when(x == 3)
    def _():
        to_row(total, tin, 3, 0, 1).wait_recv()
        begin[0], begin[1] = then(begin[0], begin[1], wide(tin))

    start_s = split(wide(begin))
    fhi[0:DK, :], flo[0:DK, :] = start_s[0][:, :DK], start_s[1][:, :DK]
    full[0:DK, :] = begin[1]
    for t in range(1, GROUP):
        y = mm(split(prefix[t - 1, 0]), start_s)
        at = slice(t * DK, (t + 1) * DK)
        fhi[at, :], flo[at, :] = split(y[:, :DK])
        full[at, :] = y[:, DK:] + prefix[t - 1, 1]

    responses(1)

    @pl.when(x == 0)
    def _():
        ein[...] = jnp.zeros_like(ein)

    @pl.when(x > 0)
    def _():
        to_row(total.at[1], ein, 1, 0, 0).wait_recv()

    @pl.when(x == 1)
    def _():
        enext[...] = mm(split(total[0]), split(ein[...])) + total[1]
        to_row(enext, ein, 3, 0, 0).start()
        to_row(enext, ein, 2, 1, 0).start()

    e_s = split(ein[...])

    y = mm((fhi[...], flo[...]), e_s) + full[...]
    for t in range(GROUP):
        staged[t] = y[t * DK:(t + 1) * DK]
    last = []
    for o in range(1, GROUP):
        p = lax.rem(place + o, GROUP)
        last.append(shared(src_ref=staged.at[p], dst_ref=arrived.at[own], send_sem=send4.at[o - 1],
                           recv_sem=recv4.at[own], device_id={"seq": base + p}))
        last[-1].start()
    arrived[own] = staged[place]
    for h in range(heads):
        @pl.when(own != h)
        def _(h=h):
            shared(src_ref=staged.at[0], dst_ref=arrived.at[h], send_sem=send4.at[0], recv_sem=recv4.at[h],
                   device_id={"seq": mirror}).wait_recv()
        cols = slice(h * DK, (h + 1) * DK)
        out[:, cols] = out[:, cols] + mm((rhi[:, cols], rlo[:, cols]), split(arrived[h]))

    for copy in [to_mirror(0), to_mirror(1)] + last:
        copy.wait_send()
    for h in range(heads):
        @pl.when(place != seats[h])
        def _(h=h):
            to_owner(h).wait_send()

    @pl.when(x == 0)
    def _():
        to_row(total.at[1], ein, 1, 0, 0).wait_send()

    @pl.when(x == 1)
    def _():
        to_row(enext, ein, 3, 0, 0).wait_send()
        to_row(enext, ein, 2, 1, 0).wait_send()

    @pl.when(x == 2)
    def _():
        to_row(total, tin, 3, 0, 1).wait_send()


def solution(mesh):
    peers, shards = mesh.shape["head"], mesh.shape["seq"]
    rows_x = shards // ZROW
    assert rows_x == 4 and shards == rows_x * ZROW

    def per_device(hid, proj, q, k, v, cq, ck, cv, scale, bias):
        heads, rows = scale.shape[0], q.shape[0]
        key_heads, blocks = q.shape[1] // DK, rows // C
        assert heads == GROUP and blocks == 4 and rows == blocks * C
        width = q.shape[1] + k.shape[1] + v.shape[1]
        per = proj.shape[1] // peers
        proj = jnp.transpose(proj)
        vm, smem = pl.BlockSpec(memory_space=pltpu.VMEM), pl.BlockSpec(memory_space=pltpu.SMEM)
        dma, pair, square = pltpu.SemaphoreType.DMA, (2, DK, DV), (C, C)

        def f32(*shape):
            return pltpu.VMEM(shape, F32)

        def result(*shape):
            return jax.ShapeDtypeStruct(shape, F32)

        def pinned(*arrays):
            return [pltpu.with_memory_space_constraint(a, pltpu.HBM) for a in arrays]

        made = pl.pallas_call(
            functools.partial(features_kernel, peers, heads),
            out_shape=(result(per, rows), result(*q.shape), result(*k.shape), result(*v.shape),
                       result(key_heads, blocks, *square), result(key_heads, blocks, *square)),
            in_specs=[vm] * 3 + [pl.BlockSpec(memory_space=pltpu.HBM)] * 5,
            out_specs=(vm,) * 6,
            scratch_shapes=[
                *(pltpu.VMEM(a.shape, BF16) for a in (hid, proj, q, k, v)), dma((5,)),
                f32(peers, per, rows), f32(peers - 1, per, rows), pltpu.VMEM((HALO, width), BF16),
                f32(rows + 8, width),
                dma((peers - 1,)), dma((peers - 1,)), dma((3,)), dma((3,)),
            ],
            compiler_params=pltpu.CompilerParams(collective_id=0, has_side_effects=True, vmem_limit_bytes=24 * 1024 * 1024),
            name="features",
        )(*pinned(cq, ck, cv, hid, proj, q, k, v))
        return pl.pallas_call(
            functools.partial(scan_kernel, heads, rows_x),
            out_shape=result(rows, heads * DV),
            in_specs=[smem] * 2 + [vm] * 6,
            out_specs=vm,
            scratch_shapes=[
                f32(heads, blocks, *square), f32(heads, blocks, C, DK + DV),
                f32(heads, blocks - 2, DK, DK + DV), f32(heads, DK, DK + DV), f32(heads, *pair),
                pltpu.VMEM((rows, heads * DK), BF16), pltpu.VMEM((rows, heads * DK), BF16),
                f32(GROUP, *pair), f32(GROUP - 1, *pair), f32(*pair), f32(*pair), f32(*pair), f32(*pair),
                f32(DK, DV), f32(*pair), f32(DK, DV), f32(GROUP * DK, DV),
                pltpu.VMEM((GROUP * DK, DK), BF16), pltpu.VMEM((GROUP * DK, DK), BF16),
                f32(GROUP, DK, DV), f32(GROUP, DK, DV),
                dma((heads,)), dma((GROUP,)), dma((2,)), dma((2,)), dma((2,)), dma((2,)),
                dma((GROUP - 1,)), dma((GROUP,)),
            ],
            compiler_params=pltpu.CompilerParams(collective_id=1, has_side_effects=True, vmem_limit_bytes=36 * 1024 * 1024),
            name="scan",
        )(*pinned(scale, bias), *made)

    placed = (
        P("seq", "head"), P("head", None), P("seq", "head"), P("seq", "head"), P("seq", "head"),
        P(None, "head"), P(None, "head"), P(None, "head"), P("head"), P("head"),
    )
    return jax.shard_map(per_device, mesh=mesh, in_specs=placed, out_specs=P("seq", "head"), check_vma=False)
```
